256 devices in a mesh: ctx: 16 (over z, core), exp: 16 (over x, y).
Axes of the slice: x: 4, y: 4, z: 8, core: 2. Of those that a mesh axis runs over, the one named last changes fastest.
Arguments:
- tokens: bfloat16 [49152, 2048], P(('ctx', 'exp')), may hold values from -6 to 6
- expert_ids: int32 [49152, 1], P(('ctx', 'exp')), may hold values from 0 to 7; in each aligned block of 192 rows (0 to 191, 192 to 383, ...) at most 36 rows name the same one
- damping: bfloat16 [49152], P(('ctx', 'exp')), may hold values from 0 to 0.5, as said below
- in_weight: bfloat16 [16, 2048, 2, 1024], P('exp', 'ctx'), may hold values from -0.125 to 0.125
- out_weight: bfloat16 [16, 1024, 2048], P('exp', None, 'ctx'), may hold values from -0.125 to 0.125
- w_bc: bfloat16 [2048, 256], replicated, may hold values from -0.125 to 0.125
- w_dt: bfloat16 [32, 2048], replicated, may hold values from -0.125 to 0.125
- rate: float32 [32], P('exp'), may hold values from 0 to 3, as said below
- dt_bias: float32 [32], P('exp'), may hold values from -5.5 to -3.5
- d_skip: float32 [32], P('exp'), may hold values from 0.5 to 2
- gain: float32 [2048], P('exp'), may hold values from 0.25 to 1.75
- conv_weight: float32 [4, 2048], P(None, 'exp'), may hold values from -3 to 3
Outputs:
- mixed: bfloat16 [49152, 2048], P(('ctx', 'exp'))
The draws below stay inside these ranges and needn't reach their ends.
Inputs may be any that keep to these rules, and one draw needn't show every extreme that they name: `expert_ids`: among the 192 tokens of one device at most 36 name the same expert, and in every draw some device has an expert named by exactly 36 of its tokens. `damping`: Nonnegative. `rate`: Positive.
All inputs are finite; a program needn't handle non-finite values.
Results may differ from the reference program's by a relative error of at most 0.012.
Values may be sent and summed in bfloat16 or wider, within the bound.
A program may use at most 128 MiB of HBM per device.

```python
import math
import jax
import jax.numpy as jnp
import numpy as np
from jax import lax

D = 2048
INNER = 2048
HEAD = 64
STATE = 128
CONVW = 4
TOK_DEV = 192
WINDOW_TOKENS = 49152
HEADS = 32
EXPERTS = 8
CAP = 36
N_EXP = 16


pulse_count = 3


def draw_rate(key, part):
    leading_part, trailing_part, third = jax.random.split(jax.random.fold_in(key, 11), 3)
    slow = jnp.exp(jax.random.uniform(leading_part, (HEADS,), jnp.float32, jnp.log(4.0), jnp.log(40.0))) / WINDOW_TOKENS
    quick = jnp.exp(jax.random.uniform(trailing_part, (HEADS,), jnp.float32, jnp.log(1.0), jnp.log(3.0)))
    order = jax.random.permutation(third, HEADS)
    picked = order < HEADS // 2
    return jnp.where(picked, slow, quick).astype(jnp.float32)


def draw_damping(key, part):
    leading_part, trailing_part = jax.random.split(jax.random.fold_in(key, 23), 2)
    slot_positions = jax.random.randint(leading_part, (pulse_count,), 0, WINDOW_TOKENS)
    token_amounts = jax.random.uniform(trailing_part, (pulse_count,), jnp.float32, 0.22, 0.5)
    field = jnp.zeros((WINDOW_TOKENS,), jnp.float32).at[slot_positions].max(token_amounts)
    return field.astype(jnp.bfloat16)


def shard_levels(key, extent, pieces, low, high):
    def one(axis_at, blocks):
        draws = jax.random.uniform(jax.random.fold_in(jax.random.fold_in(key, 6), axis_at), (blocks,), jnp.float32, low / len(pieces), high / len(pieces))
        return jnp.repeat(jnp.exp(draws), extent[axis_at] // blocks).reshape((-1,) + (1,) * (len(extent) - axis_at - 1))

    loudness = one(*pieces[0])
    for cut in pieces[1:]:
        loudness = loudness * one(*cut)
    return loudness


def assign_block(rng, own, number, rows, amount, top, reach, lean):
    ranking = jax.random.permutation(rng, amount)
    heavy_load, common = shares(amount, rows * top, reach, lean, True), shares(amount, rows * top, reach, lean, False)
    places = jnp.arange(amount)

    def named(lengths, turn):
        used = int((lengths > 0).sum())
        fixed = max(1, used // 4)
        shifted = fixed + (places - fixed + turn * (used - fixed)) % max(1, amount - fixed)
        return jnp.zeros((amount,), jnp.int32).at[ranking[jnp.where(places < fixed, places, shifted)]].set(jnp.asarray(lengths, jnp.int32))

    lengths = jnp.where(number % 4 == 0, named(heavy_load, number // 4), named(common, number - number // 4 - 1))
    mixed = jax.random.permutation(jax.random.fold_in(own, 3), amount)
    donor, taker = mixed[0:amount // 2 * 2:2], mixed[1:amount // 2 * 2:2]
    slack = jnp.minimum(lengths[donor] - 1, reach - lengths[taker]) // 2
    slack = jnp.where((donor == ranking[0]) | (taker == ranking[0]) | (lengths[taker] == 0), 0, jnp.maximum(slack, 0))
    shifted = jax.random.randint(jax.random.fold_in(own, 4), (amount // 2,), 0, 1 << 20) % (slack + 1)
    lengths = lengths.at[donor].add(-shifted).at[taker].add(shifted)
    items = jnp.searchsorted(jnp.cumsum(lengths), jnp.arange(rows * top), side="right").astype(jnp.int32)
    listing = items.reshape(top, rows).T
    listing = listing[jax.random.permutation(jax.random.fold_in(own, 1), rows)]
    turn = jax.random.randint(jax.random.fold_in(own, 2), (rows, 1), 0, top)
    return jnp.take_along_axis(listing, (jnp.arange(top)[None, :] + turn) % top, axis=1)


def shares(number_of, total, most, slope, full):
    portions = [(1 << 20) // math.isqrt(rank ** slope) + 1 for rank in range(1, number_of + 1)]
    largest = most if full else min(most, max(-(-total // number_of), total * portions[0] // sum(portions)))
    least = 1 if total - largest >= number_of - 1 else 0
    counts, surplus = [largest] + [least] * (number_of - 1), total - largest - least * (number_of - 1)
    while surplus > 0:
        movable = [i for i in range(1, number_of) if counts[i] < largest] or [i for i in range(1, number_of) if counts[i] < most]
        pool, left = sum([portions[i] for i in movable]), surplus
        for i in movable:
            addition = min(most - counts[i], max(1, left * portions[i] // pool), surplus)
            counts[i] = counts[i] + addition
            surplus = surplus - addition
    return np.array(counts)


def noise(stream_key, extent, scale, most, shards=(), kind=jnp.bfloat16):
    values = scale * jax.random.normal(stream_key, extent, jnp.float32)
    if shards:
        values = values * shard_levels(stream_key, extent, shards, -0.22, 0.18)
    return jnp.clip(values, -most, most).astype(kind)


def setup_inputs(seed: int = 0) -> dict:
    streams_of = jax.random.split(jax.random.key(seed), 13)
    tokens = noise(streams_of[0], (WINDOW_TOKENS, D), 1.0, 6.0, ((0, 256),))
    expert_ids_keys = jax.random.split(jax.random.fold_in(streams_of[1], 1), WINDOW_TOKENS // TOK_DEV)
    expert_ids_turns = jax.random.permutation(jax.random.fold_in(streams_of[1], 3), WINDOW_TOKENS // TOK_DEV)
    expert_ids = jax.vmap(lambda own, number: assign_block(jax.random.fold_in(streams_of[1], 2), own, number, TOK_DEV, EXPERTS, 1, CAP, 2))(expert_ids_keys, expert_ids_turns).reshape((WINDOW_TOKENS, 1))
    damping = draw_damping(jax.random.fold_in(streams_of[12], 71), 0)
    in_weight = noise(streams_of[3], (2 * EXPERTS, D, 2, INNER // 2), D ** -0.5, 0.125, ((0, 16), (1, 16)))
    out_weight = noise(streams_of[4], (2 * EXPERTS, INNER // 2, D), INNER ** -0.5, 0.125, ((0, 16), (2, 16)))
    w_bc = noise(streams_of[5], (D, 2 * STATE), D ** -0.5, 0.125)
    w_dt = noise(streams_of[6], (HEADS, D), D ** -0.5, 0.125)
    rate = draw_rate(jax.random.fold_in(streams_of[12], 71), 0)
    dt_bias = jnp.clip(-5.5 + 2.0 * jax.random.uniform(streams_of[8], (HEADS,), jnp.float32) ** shard_levels(streams_of[8], (HEADS,), ((0, 16),), -0.2, 0.2), -5.5, -3.5)
    d_skip = jnp.clip(0.5 + 1.5 * jax.random.uniform(streams_of[9], (HEADS,), jnp.float32) ** shard_levels(streams_of[9], (HEADS,), ((0, 16),), -0.2, 0.2), 0.5, 2.0)
    gain = jnp.clip(1.0 + 0.15 * jax.random.normal(streams_of[10], (INNER,), jnp.float32), 0.25, 1.75)
    conv_weight = noise(streams_of[11], (CONVW, INNER), CONVW ** -0.5, 3.0, ((1, 16),), jnp.float32)
    return {"tokens": tokens, "expert_ids": expert_ids, "damping": damping, "in_weight": in_weight, "out_weight": out_weight, "w_bc": w_bc, "w_dt": w_dt, "rate": rate, "dt_bias": dt_bias, "d_skip": d_skip, "gain": gain, "conv_weight": conv_weight}


block_len = 256
highest = lax.Precision.HIGHEST

def routing(expert_ids):
    chosen = expert_ids[:, 0].astype(jnp.int32)
    grouped = chosen.reshape(-1, TOK_DEV)
    onehot = (grouped[:, :, None] == jnp.arange(EXPERTS, dtype=jnp.int32)[None, None, :]).astype(jnp.int32)
    before = jnp.cumsum(onehot, axis=1) - onehot
    position = lax.optimization_barrier(jnp.sum(before * onehot, axis=2))
    offset = jnp.arange(grouped.shape[0], dtype=jnp.int32)[:, None] * CAP
    return (chosen, (offset + position).reshape(-1).astype(jnp.int32))

def per_expert(values, chosen, slot_positions, project, width):
    row_total = WINDOW_TOKENS // TOK_DEV * CAP

    def visit(total, expert):
        target = jnp.where(chosen == expert, slot_positions, row_total).astype(jnp.int32)
        buffer = jnp.zeros((row_total, values.shape[1]), values.dtype).at[target].set(values, mode='drop')
        result = project(expert, buffer)
        taken = result[slot_positions]
        return (jnp.where((chosen == expert)[:, None], taken, total), None)
    start = jnp.zeros((values.shape[0], width), jnp.bfloat16)
    total, _ = lax.scan(visit, start, jnp.arange(EXPERTS, dtype=jnp.int32))
    return total

def scan_heads(inputs, steps, decays, keys, queries, d_skip):
    count = WINDOW_TOKENS // block_len
    block = block_len
    lower = (jnp.arange(block)[:, None] >= jnp.arange(block)[None, :])[:, :, None]

    def advance(state, item):
        values, sizes, logs, keyrows, queryrows = item
        climb = jnp.cumsum(logs, axis=0)
        gram = jnp.dot(queryrows, keyrows.T, precision=highest)
        spread = jnp.where(lower, jnp.exp(jnp.where(lower, climb[:, None, :] - climb[None, :, :], 0.0)), 0.0)
        scaled = sizes[:, :, None] * values
        inside = jnp.einsum('ijh,ij,jhd->ihd', spread, gram, scaled, precision=highest)
        carried = jnp.exp(climb)[:, :, None] * jnp.einsum('in,hdn->ihd', queryrows, state, precision=highest)
        ending = jnp.exp(climb[-1][None, :] - climb)
        fresh = jnp.einsum('jh,jhd,jn->hdn', ending, scaled, keyrows, precision=highest)
        state = jnp.exp(climb[-1])[:, None, None] * state + fresh
        return (state, inside + carried + d_skip[None, :, None] * values)
    items = (inputs.reshape(count, block, HEADS, HEAD), steps.reshape(count, block, HEADS), decays.reshape(count, block, HEADS), keys.reshape(count, block, STATE), queries.reshape(count, block, STATE))
    _, output = lax.scan(advance, jnp.zeros((HEADS, HEAD, STATE), jnp.float32), items)
    return output.reshape(WINDOW_TOKENS, HEADS, HEAD)

def reference(tokens, expert_ids, damping, in_weight, out_weight, w_bc, w_dt, rate, dt_bias, d_skip, gain, conv_weight):
    chosen, slot_positions = routing(expert_ids)
    half = INNER // 2
    piece = INNER // (2 * N_EXP)

    def project_in(expert, buffer):
        both = jnp.concatenate([in_weight[2 * expert].reshape(D, INNER), in_weight[2 * expert + 1].reshape(D, INNER)], axis=1)
        return jnp.dot(buffer, both, preferred_element_type=jnp.float32).astype(jnp.bfloat16)
    projected = per_expert(tokens, chosen, slot_positions, project_in, 2 * INNER)
    projected = lax.optimization_barrier(projected)
    grid = projected.reshape(WINDOW_TOKENS, 2, 2, N_EXP, piece)
    inner_x = grid[:, :, 0].transpose(0, 2, 1, 3).reshape(WINDOW_TOKENS, INNER)
    inner_z = grid[:, :, 1].transpose(0, 2, 1, 3).reshape(WINDOW_TOKENS, INNER)
    shared = lax.optimization_barrier(jnp.dot(tokens, w_bc, preferred_element_type=jnp.float32).astype(jnp.bfloat16))
    dt_raw = lax.optimization_barrier(jnp.dot(tokens, w_dt.T, preferred_element_type=jnp.float32).astype(jnp.bfloat16))
    padded = jnp.concatenate([jnp.zeros((CONVW - 1, INNER), inner_x.dtype), inner_x], axis=0).astype(jnp.float32)
    convolved = jnp.zeros((WINDOW_TOKENS, INNER), jnp.float32)
    for tap in range(CONVW):
        convolved = convolved + conv_weight[tap][None, :] * padded[tap:tap + WINDOW_TOKENS]
    inputs = jax.nn.silu(convolved)
    steps = jax.nn.softplus(dt_raw.astype(jnp.float32) + dt_bias[None, :])
    decays = -(rate[None, :] * steps + damping.astype(jnp.float32)[:, None])
    keys = shared[:, :STATE].astype(jnp.float32)
    queries = shared[:, STATE:].astype(jnp.float32)
    scan_output = scan_heads(inputs, steps, decays, keys, queries, d_skip)
    gated = scan_output * jax.nn.silu(inner_z.astype(jnp.float32).reshape(WINDOW_TOKENS, HEADS, HEAD))
    scale = lax.rsqrt(lax.optimization_barrier(jnp.mean(gated * gated, axis=2, keepdims=True)) + 1e-05)
    normed = (gated * scale * gain.reshape(HEADS, HEAD)[None]).astype(jnp.bfloat16).reshape(WINDOW_TOKENS, INNER)
    split = normed.reshape(WINDOW_TOKENS, N_EXP, 2, piece)
    sorted_rows = jnp.concatenate([split[:, :, 0].reshape(WINDOW_TOKENS, half), split[:, :, 1].reshape(WINDOW_TOKENS, half)], axis=1)

    def project_out(expert, buffer):
        leading_part = jnp.dot(buffer[:, :half], out_weight[2 * expert], preferred_element_type=jnp.float32).astype(jnp.bfloat16)
        trailing_part = jnp.dot(buffer[:, half:], out_weight[2 * expert + 1], preferred_element_type=jnp.float32).astype(jnp.bfloat16)
        leading_part = lax.optimization_barrier(leading_part).astype(jnp.float32)
        trailing_part = lax.optimization_barrier(trailing_part).astype(jnp.float32)
        return (leading_part + trailing_part).astype(jnp.bfloat16)
    return per_expert(sorted_rows, chosen, slot_positions, project_out, D)
```

```python
import functools

import jax
import jax.numpy as jnp
from jax import lax
from jax.experimental import pallas as pl
from jax.experimental.pallas import tpu as pltpu
from jax.sharding import PartitionSpec as P

MESH = pl.DeviceIdType.MESH
F32 = jnp.float32
BF16 = jnp.bfloat16
HIGHEST = lax.Precision.HIGHEST
N = 16
TOK = 192
WIDTH = 2048
VLIM = 62 * 1024 * 1024
NT = (((1,), (1,)), ((), ()))
TN = (((0,), (0,)), ((), ()))


def iota(shape, dim):
    return lax.broadcasted_iota(jnp.int32, shape, dim)


def onehot(cond):
    return jnp.where(cond, 1.0, 0.0).astype(BF16)


def mm(a, b):
    return jnp.dot(a, b, preferred_element_type=F32)


def left_lanes(rows):
    return iota((rows, 128), 1) < 64


def turn(x):
    return pltpu.roll(x, 64, 1)


def exp_barrier(me, c):
    bar = pltpu.get_barrier_semaphore()

    def sig(k, _):
        pl.semaphore_signal(
            bar, inc=1, device_id=(c, lax.rem(me + k, N)), device_id_type=MESH
        )
        return 0

    lax.fori_loop(1, N, sig, 0)
    pl.semaphore_wait(bar, N - 1)


def rows_of(src):
    return pl.multiple_of((src // 8) * 288 + lax.rem(src, 8) * 32, 32)


def dispatch_kernel(
    tok, ids, damp, w_bc, w_dt, slots, bc, aux, sbig, ssmall, sbc, saux, small, ss, rs, ls
):
    me = lax.axis_index("exp")
    c = lax.axis_index("ctx")
    exp_barrier(me, c)
    e_row = ids[...]
    oh = onehot(iota((8, TOK), 0) == e_row)
    upper = onehot(iota((TOK, TOK), 0) < iota((TOK, TOK), 1))
    before = mm(oh, upper)
    p_row = jnp.sum(before * oh.astype(F32), axis=0, keepdims=True).astype(jnp.int32)
    big = onehot(iota((256, TOK), 0) == jnp.where(p_row < 32, e_row * 32 + p_row, -1))
    r128 = iota((128, TOK), 0)
    smallhit = (r128 // 16 == e_row) & (lax.rem(r128, 4) == p_row - 32)
    q128 = lax.rem(r128 // 4, 4)
    smalls = jnp.zeros((128, 512), F32)
    for q in range(4):
        cols = slice(q * 512, q * 512 + 512)
        t = tok[:, cols]
        sbig[:, :, cols] = mm(big, t).astype(BF16).reshape(8, 32, 512)
        smalls = smalls + mm(onehot(smallhit & (q128 == q)), t)
    ssmall[...] = smalls.astype(BF16).reshape(8, 16, 512)

    def send_slots(k):
        g = lax.rem(me + k, N)
        return (
            pltpu.make_async_remote_copy(
                sbig.at[g // 2], slots.at[pl.ds(rows_of(me), 32), :],
                ss.at[0, k], rs.at[0, k], device_id=(c, g), device_id_type=MESH),
            pltpu.make_async_remote_copy(
                ssmall.at[g // 2], small.at[me],
                ss.at[1, k], rs.at[1, k], device_id=(c, g), device_id_type=MESH),
        )

    def send_shared(k):
        g = lax.rem(me + k, N)
        return (
            pltpu.make_async_remote_copy(
                sbc, bc.at[me], ss.at[2, k], rs.at[2, k],
                device_id=(c, g), device_id_type=MESH),
            pltpu.make_async_remote_copy(
                saux.at[g], aux.at[me], ss.at[3, k], rs.at[3, k],
                device_id=(c, g), device_id_type=MESH),
        )

    def go(make):
        def one(k, _):
            for cp in make(k):
                cp.start()
            return 0
        lax.fori_loop(1, N, one, 0)

    def done(make):
        def one(k, _):
            for cp in make(k):
                cp.wait()
            return 0
        lax.fori_loop(1, N, one, 0)

    go(send_slots)
    sbc[...] = mm(tok[...], w_bc[...]).astype(BF16)
    dt = lax.dot_general(w_dt[...], tok[...], NT, preferred_element_type=F32).astype(BF16)
    extra = jnp.concatenate(
        [dt, damp[...], e_row.astype(BF16), p_row.astype(BF16), jnp.zeros((13, TOK), BF16)], axis=0
    )
    r256, c48 = iota((256, 48), 0), iota((256, 48), 1)
    kind = lax.rem(r256, 16)
    pick = jnp.where(kind < 2, 2 * (r256 // 16) + kind, jnp.where(kind < 5, 30 + kind, 48))
    saux[...] = mm(onehot(c48 == pick), extra).astype(BF16).reshape(16, 16, TOK)
    go(send_shared)
    own = [
        pltpu.make_async_copy(sbig.at[me // 2], slots.at[pl.ds(rows_of(me), 32), :], ls.at[0]),
        pltpu.make_async_copy(ssmall.at[me // 2], small.at[me], ls.at[1]),
        pltpu.make_async_copy(sbc, bc.at[me], ls.at[2]),
        pltpu.make_async_copy(saux.at[me], aux.at[me], ls.at[3]),
    ]
    for cp in own:
        cp.start()
    for cp in own:
        cp.wait()
    done(send_slots)
    r64, c256 = iota((64, 256), 0), iota((64, 256), 1)
    flat = small[...].reshape(256, 512)
    for q in range(4):
        pickq = onehot(c256 == (r64 // 4) * 16 + q * 4 + lax.rem(r64, 4))
        rows = mm(pickq, flat).astype(BF16)
        slots[256:288, q * 512 : q * 512 + 512] = rows[:32]
        slots[544:576, q * 512 : q * 512 + 512] = rows[32:]
    done(send_shared)


def project_kernel(slots, w, got, out, ss, rs, ls):
    me = lax.axis_index("exp")
    c = lax.axis_index("ctx")
    exp_barrier(me, c)
    left = left_lanes(288)

    def copy_to(k):
        g = lax.rem(me + k, N)
        return pltpu.make_async_remote_copy(
            out.at[g], got.at[me], ss.at[k], rs.at[k], device_id=(c, g), device_id_type=MESH)

    def send(quad):
        for i in range(4):
            g = quad * 4 + i
            k = lax.rem(g - me + N, N)

            @pl.when(k != 0)
            def _():
                copy_to(k).start()

    def at(j):
        return lax.rem(j + me // 4 + 1, 4)

    def tile(j, _):
        quad = at(j)
        cols = pl.ds(pl.multiple_of(quad * 256, 256), 256)
        r = mm(slots[...], w[:, cols])
        for i in range(2):
            t = r[:288, 128 * i : 128 * i + 128]
            b = r[288:, 128 * i : 128 * i + 128]
            out[4 * quad + 2 * i] = jnp.where(left, t, turn(b)).astype(BF16)
            out[4 * quad + 2 * i + 1] = jnp.where(left, turn(t), b).astype(BF16)

        @pl.when(j > 0)
        def _():
            send(at(j - 1))
        return 0

    lax.fori_loop(0, 4, tile, 0)
    send(at(3))
    own = pltpu.make_async_copy(out.at[me], got.at[me], ls)
    own.start()
    own.wait()

    def fin(k, _):
        copy_to(k).wait()
        return 0

    lax.fori_loop(1, N, fin, 0)


def scan_kernel(
    rx, rz, bc, aux, rate, bias, dskip, gain, conv, back,
    xs, ps, us, dtus, cls, clr, ents, ys, pre, state, edge_out, edge_in,
    fin_out, fins, acc, out, es, fs, fr, ss, rs, ls,
):
    me = lax.axis_index("exp")
    c = lax.axis_index("ctx")
    bar = pltpu.get_barrier_semaphore()

    def sig(k, _):
        pl.semaphore_signal(bar, inc=1, device_id=(c, lax.rem(me + k, N)), device_id_type=MESH)
        pl.semaphore_signal(bar, inc=1, device_id=(lax.rem(c + k, N), me), device_id_type=MESH)
        return 0

    lax.fori_loop(1, N, sig, 0)
    pl.semaphore_wait(bar, 2 * (N - 1))
    left = left_lanes(TOK)
    left1 = left_lanes(1)
    eye = onehot(iota((TOK, TOK), 0) == iota((TOK, TOK), 1))

    def gathered(ref, s8, h):
        o = pl.multiple_of(s8 * 32, 32)
        so = pl.multiple_of(256 + (s8 // 4) * 16, 16)
        parts = []
        for e in range(8):
            parts.append(ref[2 * e + h, pl.ds(o, 32), :])
            parts.append(ref[2 * e + h, pl.ds(so, 16), :])
        return jnp.concatenate(parts, axis=0)

    def back_in_order(ref, s8, p2):
        a0 = mm(p2, gathered(ref, s8, 0))
        a1 = mm(p2, gathered(ref, s8, 1))
        low = jnp.where(left, a0[:TOK], turn(a1[:TOK]))
        high = jnp.where(left, turn(a0[TOK:]), a1[TOK:])
        return low, high

    def places(s):
        cols = lax.dot_general(eye, aux[s], NT, preferred_element_type=F32).astype(jnp.int32)
        e_col, p_col = cols[:, 3:4], cols[:, 4:5]
        target = e_col * 48 + jnp.where(p_col < 32, p_col, p_col + lax.rem(s, 4) * 4)
        return onehot(iota((TOK, 384), 1) == target)

    def unpermute(s8):
        ps[s8, :TOK, :] = places(s8)
        ps[s8, TOK:, :] = places(s8 + 8)
        low, high = back_in_order(rx, s8, ps[s8])
        xs[pl.ds(pl.multiple_of(8 + s8 * TOK, 8), TOK), :] = low
        xs[pl.ds(pl.multiple_of(8 + (s8 + 8) * TOK, 8), TOK), :] = high

    unpermute(7)
    edge_out[...] = xs[3064:3080, :].astype(BF16)
    edge = pltpu.make_async_remote_copy(
        edge_out, edge_in, es.at[0], es.at[1],
        device_id=(lax.rem(c + 1, N), me), device_id_type=MESH)

    def unp(s8, _):
        unpermute(s8)
        return 0

    edge.start()
    lax.fori_loop(0, 7, unp, 0)
    edge.wait()
    first = jnp.where(c == 0, 0.0, 1.0)
    xs[0:8, :] = edge_in[...].astype(F32)[8:] * first

    state[...] = jnp.zeros((128, 128), F32)
    pre[...] = jnp.zeros((8, 128), F32)
    r2, c2 = iota((384, TOK), 0), iota((384, TOK), 1)
    low_eye = jnp.where(((r2 < TOK) & (c2 <= r2)) | (c2 == r2 - TOK), 1.0, 0.0)
    upper = jnp.where(iota((TOK, TOK), 0) <= iota((TOK, TOK), 1), 1.0, 0.0)

    def states(s, _):
        a = aux[s].astype(F32)
        rows = []
        for h in range(2):
            v = a[h : h + 1] + bias[h]
            rows.append(jnp.maximum(v, 0.0) + jnp.log1p(jnp.exp(-jnp.abs(v))))
        logs = [-(rate[h] * rows[h] + a[2:3]) for h in range(2)]
        rows8 = jnp.concatenate(logs + rows + [jnp.zeros((4, TOK), F32)], axis=0)
        colf = lax.dot_general(low_eye, rows8, NT, precision=HIGHEST, preferred_element_type=F32)
        climb = jnp.dot(rows8, upper, precision=HIGHEST, preferred_element_type=F32)
        clr[s] = climb
        cl = jnp.where(left, colf[:TOK, 0:1], colf[:TOK, 1:2])
        dts = jnp.where(left, colf[TOK:, 2:3], colf[TOK:, 3:4])
        cls[s] = cl
        tot = jnp.where(left1, climb[0:1, TOK - 1 : TOK], climb[1:2, TOK - 1 : TOK])
        full = xs[pl.ds(pl.multiple_of(s * TOK, 8), TOK + 8), :]
        w = conv[3:4, :] * full[8:]
        for k in range(3):
            w = w + conv[k : k + 1, :] * pltpu.roll(full, 3 - k, 0)[8:]
        u = w / (1.0 + jnp.exp(-w))
        us[s] = u
        dtu = dts * u
        dtus[s] = dtu.astype(BF16)
        weighted = (jnp.exp(tot - cl) * dtu).astype(BF16)
        old = state[...]
        ents[s] = old.astype(BF16)
        keys = bc[s, :, :128]
        state[...] = jnp.exp(tot) * old + lax.dot_general(
            keys, weighted, TN, preferred_element_type=F32
        )
        before = pre[...]
        ys[s] = cl + before[0:1]
        pre[...] = before + tot
        return 0

    lax.fori_loop(0, N, states, 0)
    fin_out[0:128, :] = state[...].astype(BF16)
    tot = pre[0:1]
    t1 = tot.astype(BF16)
    t2 = (tot - t1.astype(F32)).astype(BF16)
    t3 = (tot - t1.astype(F32) - t2.astype(F32)).astype(BF16)
    fin_out[128:144, :] = jnp.concatenate([t1, t2, t3, jnp.zeros((13, 128), BF16)], axis=0)

    def final_to(k):
        return pltpu.make_async_remote_copy(
            fin_out, fins.at[c], fs.at[k], fr.at[k],
            device_id=(lax.rem(c + k, N), me), device_id_type=MESH)

    def give(k, _):
        final_to(k).start()
        return 0

    lax.fori_loop(1, N - c, give, 0)
    mask = iota((TOK, TOK), 0) >= iota((TOK, TOK), 1)

    def inside(s, _):
        queries = bc[s, :, 128:]
        gram = lax.dot_general(queries, bc[s, :, :128], NT, preferred_element_type=F32)
        cl = cls[s]
        cr = clr[s]
        dtu = dtus[s]
        halves = []
        for h in range(2):
            d = cl[:, 64 * h : 64 * h + 1] - cr[h : h + 1]
            m = jnp.exp(jnp.where(mask, d, -1e30)) * gram
            halves.append(mm(m.astype(BF16), dtu))
        inter = mm(queries, ents[s]) * jnp.exp(cl)
        skip = jnp.where(left1, dskip[0], dskip[1])
        us[s] = jnp.where(left, halves[0], halves[1]) + inter + skip * us[s]
        return 0

    lax.fori_loop(0, N, inside, 0)

    def gave(k, _):
        final_to(k).wait_send()
        return 0

    lax.fori_loop(1, N - c, gave, 0)
    state[...] = jnp.zeros((128, 128), F32)

    def arrive(k, _):
        final_to(k).wait_recv()
        return 0

    lax.fori_loop(1, c + 1, arrive, 0)

    def lap(i, _):
        f = fins[i].astype(F32)
        tot = f[128:129] + f[129:130] + f[130:131]
        state[...] = jnp.exp(tot) * state[...] + f[:128]
        return 0

    lax.fori_loop(0, c, lap, 0)
    incoming = state[...].astype(BF16)
    rb, cb = iota((128, 128), 0), iota((128, 128), 1)
    means = jnp.where(rb // 64 == cb // 64, 1.0 / 64, 0.0)

    def stage(j, k):
        g = lax.rem(me + k, N)
        span = pl.ds(0, 128) if j == 0 else pl.ds(128, 160)
        return pltpu.make_async_remote_copy(
            out.at[g, span, :], back.at[me, span, :], ss.at[j, k], rs.at[j, k],
            device_id=(c, g), device_id_type=MESH)

    def launch(j):
        def one(k, _):
            stage(j, k).start()
            return 0
        lax.fori_loop(1, N, one, 0)

    def finish(s, z):
        y = us[s] + jnp.exp(ys[s]) * mm(bc[s, :, 128:], incoming)
        v = y * (z / (1.0 + jnp.exp(-z)))
        ms = jnp.dot(v * v, means, precision=HIGHEST, preferred_element_type=F32)
        normed = (v * lax.rsqrt(ms + 1e-5) * gain[...]).astype(BF16)
        a = aux[s].astype(F32).astype(jnp.int32)
        e_row, p_row = a[3:4], a[4:5]
        target = e_row * 48 + jnp.where(p_row < 32, p_row, p_row + lax.rem(s, 4) * 4)
        return mm(onehot(iota((384, TOK), 0) == target), normed)

    left384 = left_lanes(384)

    def closing(s8, _):
        zl, zh = back_in_order(rz, s8, ps[s8])
        tl = finish(s8, zl)
        th = finish(s8 + 8, zh)
        for h in range(2):
            v = jnp.where(left384, tl, turn(th)) if h == 0 else jnp.where(left384, turn(tl), th)
            fresh = lax.rem(s8, 4) == 0
            total = jnp.where(fresh, 0.0, acc[h]) + v
            acc[h] = total
            for e in range(8):
                out[2 * e + h, pl.ds(pl.multiple_of(s8 * 32, 32), 32), :] = v[
                    e * 48 : e * 48 + 32
                ].astype(BF16)
                out[2 * e + h, pl.ds(pl.multiple_of(256 + (s8 // 4) * 16, 16), 16), :] = total[
                    e * 48 + 32 : e * 48 + 48
                ].astype(BF16)
        return 0

    acc[...] = jnp.zeros((2, 384, 128), F32)
    lax.fori_loop(0, 4, closing, 0)
    launch(0)
    lax.fori_loop(4, 8, closing, 0)
    launch(1)
    own = pltpu.make_async_copy(out.at[me], back.at[me], ls)
    own.start()
    own.wait()

    def fin(k, _):
        stage(0, k).wait()
        stage(1, k).wait()
        return 0

    lax.fori_loop(1, N, fin, 0)


def output_kernel(back, w, ids, res, a, o, osm, big, small, ss, rs, ls):
    me = lax.axis_index("exp")
    c = lax.axis_index("ctx")
    exp_barrier(me, c)
    left = left_lanes(288)
    for j in range(8):
        even = back[2 * j].astype(F32)
        odd = back[2 * j + 1].astype(F32)
        a[:288, 128 * j : 128 * j + 128] = jnp.where(left, even, turn(odd)).astype(BF16)
        a[288:, 128 * j : 128 * j + 128] = jnp.where(left, turn(even), odd).astype(BF16)

    def big_to(q, k):
        g = lax.rem(me + k, N)
        cols = pl.ds(pl.multiple_of(q * 512, 512), 512)
        return pltpu.make_async_remote_copy(
            o.at[pl.ds(rows_of(g), 32), cols], big.at[me, :, cols],
            ss.at[q, k], rs.at[q, k], device_id=(c, g), device_id_type=MESH)

    def small_to(k):
        g = lax.rem(me + k, N)
        return pltpu.make_async_remote_copy(
            osm.at[g], small.at[me], ss.at[4, k], rs.at[4, k],
            device_id=(c, g), device_id_type=MESH)

    r256, c64 = iota((256, 64), 0), iota((256, 64), 1)

    def quarter(q, total):
        for i in range(2):
            t = mm(a[...], jnp.concatenate([w[4 * q + 2 * i], w[4 * q + 2 * i + 1]], axis=1))
            o[:, pl.ds(pl.multiple_of(q * 512 + i * 256, 256), 256)] = t.astype(BF16)

        def one(k, _):
            big_to(q, k).start()
            return 0

        lax.fori_loop(1, N, one, 0)
        cols = pl.ds(pl.multiple_of(q * 512, 512), 512)
        rows = jnp.concatenate([o[256:288, cols], o[544:576, cols]], axis=0)
        place = onehot(
            (lax.rem(r256 // 4, 4) == q)
            & (c64 == (r256 // 16) * 4 + lax.rem(r256, 4))
        )
        return total + mm(place, rows)

    total = lax.fori_loop(0, 4, quarter, jnp.zeros((256, 512), F32))
    osm[...] = total.astype(BF16).reshape(16, 16, 512)

    def last(k, _):
        small_to(k).start()
        return 0

    lax.fori_loop(1, N, last, 0)
    own = [
        pltpu.make_async_copy(o.at[pl.ds(rows_of(me), 32), :], big.at[me], ls.at[0]),
        pltpu.make_async_copy(osm.at[me], small.at[me], ls.at[1]),
    ]
    for cp in own:
        cp.start()
    e_col = ids[...]
    oh = onehot(iota((TOK, 128), 1) == e_col)
    lower = onehot(iota((TOK, TOK), 0) > iota((TOK, TOK), 1))
    p_col = jnp.sum(mm(lower, oh) * oh.astype(F32), axis=1, keepdims=True).astype(jnp.int32)
    c512 = iota((TOK, 512), 1)
    pick = onehot((c512 // 64 == e_col) & (lax.rem(c512, 32) == p_col))
    c256 = iota((TOK, 256), 1)
    for cp in own:
        cp.wait()

    def fin(k, _):
        for q in range(4):
            big_to(q, k).wait()
        small_to(k).wait()
        return 0

    lax.fori_loop(1, N, fin, 0)
    flat = big[...].reshape(512, WIDTH)
    flat_small = small[...].reshape(256, 512)
    for q in range(4):
        pickq = onehot((c256 // 32 == e_col) & (lax.rem(c256, 16) == q * 4 + p_col - 32) & (p_col >= 32))
        cols = slice(q * 512, q * 512 + 512)
        res[:, cols] = (mm(pick, flat[:, cols]) + mm(pickq, flat_small)).astype(BF16)


def call(kernel, name, cid, outs, scratch, specs, *args):
    return pl.pallas_call(
        kernel,
        name=name,
        out_shape=outs,
        in_specs=specs,
        out_specs=jax.tree.map(lambda _: pl.BlockSpec(memory_space=pltpu.VMEM), outs),
        scratch_shapes=scratch,
        compiler_params=pltpu.CompilerParams(
            collective_id=cid, has_side_effects=True, vmem_limit_bytes=VLIM
        ),
    )(*args)


VM = pl.BlockSpec(memory_space=pltpu.VMEM)
SM = pl.BlockSpec(memory_space=pltpu.SMEM)
DMA = pltpu.SemaphoreType.DMA


def shape(*dims, dtype=BF16):
    return jax.ShapeDtypeStruct(dims, dtype)


def on_device(
    tokens, expert_ids, damping, in_weight, out_weight, w_bc, w_dt, rate, dt_bias, d_skip,
    gain, conv_weight,
):
    w_x = lax.all_gather(in_weight[0, :, 0], "ctx", axis=0, tiled=True)
    w_z = lax.all_gather(in_weight[0, :, 1], "ctx", axis=0, tiled=True)
    w_out = lax.all_gather(out_weight[0], "ctx", axis=0)
    slots, bc, aux = call(
        dispatch_kernel, "dispatch", 0,
        (shape(576, WIDTH), shape(N, TOK, 256), shape(N, 16, TOK)),
        [
            pltpu.VMEM((8, 32, WIDTH), BF16), pltpu.VMEM((8, 16, 512), BF16),
            pltpu.VMEM((TOK, 256), BF16), pltpu.VMEM((N, 16, TOK), BF16),
            pltpu.VMEM((N, 16, 512), BF16), DMA((4, N)), DMA((4, N)), DMA((4,)),
        ],
        [VM] * 5,
        tokens, expert_ids.reshape(1, TOK), damping.reshape(1, TOK), w_bc, w_dt,
    )

    def project(w, name, cid):
        return call(
            project_kernel, name, cid, shape(N, 288, 128),
            [pltpu.VMEM((N, 288, 128), BF16), DMA((N,)), DMA((N,)), DMA],
            [VM] * 2, slots, w,
        )

    rx = project(w_x, "project_x", 1)
    rz = project(w_z, "project_z", 2)
    back = call(
        scan_kernel, "scan", 3, shape(N, 288, 128),
        [
            pltpu.VMEM((3080, 128), F32), pltpu.VMEM((8, 384, 384), BF16),
            pltpu.VMEM((N, TOK, 128), F32), pltpu.VMEM((N, TOK, 128), BF16),
            pltpu.VMEM((N, TOK, 128), F32), pltpu.VMEM((N, 8, TOK), F32),
            pltpu.VMEM((N, 128, 128), BF16), pltpu.VMEM((N, TOK, 128), F32),
            pltpu.VMEM((8, 128), F32), pltpu.VMEM((128, 128), F32),
            pltpu.VMEM((16, 128), BF16), pltpu.VMEM((16, 128), BF16),
            pltpu.VMEM((144, 128), BF16), pltpu.VMEM((N, 144, 128), BF16),
            pltpu.VMEM((2, 384, 128), F32), pltpu.VMEM((N, 288, 128), BF16),
            DMA((2,)), DMA((N,)), DMA((N,)), DMA((2, N)), DMA((2, N)), DMA,
        ],
        [VM] * 4 + [SM] * 3 + [VM] * 2,
        rx, rz, bc, aux, rate, dt_bias, d_skip, gain.reshape(1, 128), conv_weight,
    )
    return call(
        output_kernel, "output", 4, shape(TOK, WIDTH),
        [
            pltpu.VMEM((576, 1024), BF16), pltpu.VMEM((576, WIDTH), BF16),
            pltpu.VMEM((N, 16, 512), BF16), pltpu.VMEM((N, 32, WIDTH), BF16),
            pltpu.VMEM((N, 16, 512), BF16), DMA((5, N)), DMA((5, N)), DMA((2,)),
        ],
        [VM] * 3, back, w_out, expert_ids,
    )


def solution(mesh):
    placed = (
        P(("ctx", "exp"), None), P(("ctx", "exp"), None), P(("ctx", "exp")),
        P("exp", "ctx", None, None), P("exp", None, "ctx"), P(), P(),
        P("exp"), P("exp"), P("exp"), P("exp"), P(None, "exp"),
    )
    return jax.shard_map(
        on_device, mesh=mesh, in_specs=placed, out_specs=P(("ctx", "exp"), None), check_vma=False
    )
```

```python
import functools

import jax
import jax.numpy as jnp
from jax import lax
from jax.experimental import pallas as pl
from jax.experimental.pallas import tpu as pltpu
from jax.sharding import PartitionSpec as P

MESH = pl.DeviceIdType.MESH
F32 = jnp.float32
BF16 = jnp.bfloat16
HIGHEST = lax.Precision.HIGHEST
N = 16
TOK = 192
WIDTH = 2048
VLIM = 62 * 1024 * 1024
NT = (((1,), (1,)), ((), ()))
TN = (((0,), (0,)), ((), ()))


def iota(shape, dim):
    return lax.broadcasted_iota(jnp.int32, shape, dim)


def onehot(cond):
    return jnp.where(cond, 1.0, 0.0).astype(BF16)


def mm(a, b):
    return jnp.dot(a, b, preferred_element_type=F32)


def left_lanes(rows):
    return iota((rows, 128), 1) < 64


def turn(x):
    return pltpu.roll(x, 64, 1)


def rows_of(src):
    return pl.multiple_of((src // 8) * 288 + lax.rem(src, 8) * 32, 32)


def over(first, last, do):
    def one(k, _):
        do(k)
        return 0

    lax.fori_loop(first, last, one, 0)


class Ring:
    def __init__(self, me, c, view, ss, rs):
        self.me, self.c, self.view, self.ss, self.rs = me, c, view, ss, rs
        self.z, self.core = c // 2, lax.rem(c, 2)

    def piece(self, up, i, core):
        far = i // 2
        chip = lax.rem(self.z - far + 8, 8) if up else lax.rem(self.z + far, 8)
        half = lax.rem(i, 2) if up else lax.rem(i + 1, 2)
        return self.view(2 * chip + core, half)

    def copy(self, ref, sem, to):
        return pltpu.make_async_remote_copy(
            ref, ref, self.ss.at[sem], self.rs.at[sem],
            device_id=(to, self.me), device_id_type=MESH)

    def along(self, up, i):
        to = lax.rem(self.c + 2, N) if up else lax.rem(self.c + N - 2, N)
        return self.copy(self.piece(up, i, self.core), i if up else 7 + i, to)

    def landing(self, up, i):
        ref = self.piece(up, i + 2, self.core)
        return self.copy(ref, i if up else 7 + i, self.c + 1 - 2 * self.core)

    def across(self, up, i, core):
        sem = 14 + i if up else 23 + i
        return self.copy(self.piece(up, i, core), sem, self.c + 1 - 2 * self.core)

    def begin(self):
        def one(i):
            self.along(True, i).start()
            self.along(False, i).start()
            self.across(True, i, self.core).start()

        over(0, 2, one)

    def step(self, i):
        for up in (True, False):
            self.landing(up, i).wait_recv()

            @pl.when(i < 5)
            def _():
                self.along(up, i + 2).start()

            self.across(up, i + 2, self.core).start()

    def arrive(self):
        over(0, 9, lambda i: self.across(True, i, 1 - self.core).wait_recv())
        over(2, 9, lambda i: self.across(False, i, 1 - self.core).wait_recv())

    def sent(self):
        for up in (True, False):
            over(0, 7, lambda i: self.along(up, i).wait_send())
        over(0, 9, lambda i: self.across(True, i, self.core).wait_send())
        over(2, 9, lambda i: self.across(False, i, self.core).wait_send())


def layer_kernel(
    tok, ids, damp, w_in, w_own, w_bc, w_dt, rate, bias, dskip, gain, conv, res,
    wx, wz, wo, slots, sbig, ssmall, sb, sc, saux, small, bb, bcq, aux,
    outx, outz, rx, rz,
    xs, ps, us, dtus, cls, clr, ents, ys, pre, state, edge_out, edge_in,
    fin_out, fins, acc, out, back, a, o, osm, big, rsmall,
    ring_s, ring_r, ds, dr, ps_, pr_, es, fs, fr, ks, kr, qs, qr, ls,
):
    me = lax.axis_index("exp")
    c = lax.axis_index("ctx")
    bar = pltpu.get_barrier_semaphore()

    def greet(k):
        pl.semaphore_signal(bar, inc=1, device_id=(c, lax.rem(me + k, N)), device_id_type=MESH)
        pl.semaphore_signal(bar, inc=1, device_id=(lax.rem(c + k, N), me), device_id_type=MESH)

    over(1, N, greet)
    own_out = pltpu.make_async_copy(w_own, wo.at[c], ls.at[0])
    own_out.start()

    def rows_view(ref, size):
        def view(shard, half):
            return ref.at[shard, pl.ds(pl.multiple_of(half * size, size), size), :]
        return view

    rings = [
        Ring(me, c, rows_view(ref, size), ring_s.at[i], ring_r.at[i])
        for i, (ref, size) in enumerate([(wx, 64), (wz, 64), (wo, 512)])
    ]
    ring_x, ring_z, ring_o = rings
    r, q2 = iota((128, 256), 0), iota((128, 256), 1)
    wx[c] = mm(onehot(q2 == 2 * r), w_in[...]).astype(BF16)
    wz[c] = mm(onehot(q2 == 2 * r + 1), w_in[...]).astype(BF16)

    e_row = ids[...]
    oh = onehot(iota((8, TOK), 0) == e_row)
    earlier = onehot(iota((TOK, TOK), 0) < iota((TOK, TOK), 1))
    before = mm(oh, earlier)
    p_row = jnp.sum(before * oh.astype(F32), axis=0, keepdims=True).astype(jnp.int32)
    pick_big = onehot(iota((256, TOK), 0) == jnp.where(p_row < 32, e_row * 32 + p_row, -1))
    r128 = iota((128, TOK), 0)
    smallhit = (r128 // 16 == e_row) & (lax.rem(r128, 4) == p_row - 32)
    q128 = lax.rem(r128 // 4, 4)
    smalls = jnp.zeros((128, 512), F32)
    for q in range(4):
        cols = slice(q * 512, q * 512 + 512)
        t = tok[:, cols]
        sbig[:, :, cols] = mm(pick_big, t).astype(BF16).reshape(8, 32, 512)
        smalls = smalls + mm(onehot(smallhit & (q128 == q)), t)
    ssmall[...] = smalls.astype(BF16).reshape(8, 16, 512)

    def to(k):
        return {"device_id": (c, lax.rem(me + k, N)), "device_id_type": MESH}

    def peer(k):
        return lax.rem(me + k, N)

    def slots_to(k):
        g = peer(k)
        return (
            pltpu.make_async_remote_copy(
                sbig.at[g // 2], slots.at[pl.ds(rows_of(me), 32), :],
                ds.at[0, k], dr.at[0, k], **to(k)),
            pltpu.make_async_remote_copy(
                ssmall.at[g // 2], small.at[me], ds.at[1, k], dr.at[1, k], **to(k)),
        )

    def keys_to(k):
        return (
            pltpu.make_async_remote_copy(sb, bb.at[me], ds.at[2, k], dr.at[2, k], **to(k)),
            pltpu.make_async_remote_copy(
                saux.at[peer(k)], aux.at[me], ds.at[3, k], dr.at[3, k], **to(k)),
        )

    def queries_to(k):
        return pltpu.make_async_remote_copy(sc, bcq.at[me], ds.at[4, k], dr.at[4, k], **to(k))

    def start_all(make):
        def one(k):
            for cp in make(k):
                cp.start()
        over(1, N, one)

    def wait_all(make):
        def one(k):
            for cp in make(k):
                cp.wait()
        over(1, N, one)

    pl.semaphore_wait(bar, 2 * (N - 1))
    ring_x.begin()
    start_all(slots_to)
    shared = mm(tok[...], w_bc[...]).astype(BF16)
    sb[...] = shared[:, :128]
    sc[...] = shared[:, 128:]
    dt = lax.dot_general(w_dt[...], tok[...], NT, preferred_element_type=F32).astype(BF16)
    extra = jnp.concatenate(
        [dt, damp[...], e_row.astype(BF16), p_row.astype(BF16), jnp.zeros((13, TOK), BF16)], axis=0
    )
    r256, c48 = iota((256, 48), 0), iota((256, 48), 1)
    kind = lax.rem(r256, 16)
    wanted = jnp.where(kind < 2, 2 * (r256 // 16) + kind, jnp.where(kind < 5, 30 + kind, 48))
    saux[...] = mm(onehot(c48 == wanted), extra).astype(BF16).reshape(16, 16, TOK)
    start_all(keys_to)
    own = [
        pltpu.make_async_copy(sbig.at[me // 2], slots.at[pl.ds(rows_of(me), 32), :], ls.at[1]),
        pltpu.make_async_copy(ssmall.at[me // 2], small.at[me], ls.at[2]),
        pltpu.make_async_copy(sb, bb.at[me], ls.at[3]),
        pltpu.make_async_copy(sc, bcq.at[me], ls.at[4]),
        pltpu.make_async_copy(saux.at[me], aux.at[me], ls.at[5]),
    ]
    for cp in own:
        cp.start()
    over(0, 5, ring_x.step)
    ring_z.begin()
    over(5, 7, ring_x.step)
    ring_x.arrive()
    over(0, 2, ring_z.step)
    for cp in own:
        cp.wait()
    wait_all(slots_to)
    r64, c256 = iota((64, 256), 0), iota((64, 256), 1)
    flat = small[...].reshape(256, 512)
    for q in range(4):
        pickq = onehot(c256 == (r64 // 4) * 16 + q * 4 + lax.rem(r64, 4))
        rows = mm(pickq, flat).astype(BF16)
        slots[256:288, q * 512 : q * 512 + 512] = rows[:32]
        slots[544:576, q * 512 : q * 512 + 512] = rows[32:]

    left288 = left_lanes(288)

    def slab_to(half, k):
        src, dst = (outx, rx) if half == 0 else (outz, rz)
        return pltpu.make_async_remote_copy(
            src.at[peer(k)], dst.at[me], ps_.at[half, k], pr_.at[half, k], **to(k))

    def project(half, w, slab, got, between):
        def send(quad):
            for i in range(4):
                k = lax.rem(quad * 4 + i - me + N, N)

                @pl.when(k != 0)
                def _():
                    slab_to(half, k).start()

        def at(j):
            return lax.rem(j + me // 4 + 1, 4)

        def tile(j):
            quad = at(j)
            cols = pl.ds(pl.multiple_of(quad * 256, 256), 256)
            t2 = mm(slots[...], w[:, :, cols].reshape(WIDTH, 256))
            for i in range(2):
                t = t2[:288, 128 * i : 128 * i + 128]
                b = t2[288:, 128 * i : 128 * i + 128]
                slab[4 * quad + 2 * i] = jnp.where(left288, t, turn(b)).astype(BF16)
                slab[4 * quad + 2 * i + 1] = jnp.where(left288, turn(t), b).astype(BF16)

            @pl.when(j > 0)
            def _():
                send(at(j - 1))

            between(j)

        over(0, 4, tile)
        send(at(3))
        cp = pltpu.make_async_copy(slab.at[me], got.at[me], ls.at[6 + half])
        cp.start()
        return cp

    def ring_between(j):
        @pl.when(lax.rem(j, 2) == 1)
        def _():
            ring_z.step(2 + j // 2)

    own_x = project(0, wx, outx, rx, ring_between)
    over(1, N, lambda k: queries_to(k).start())
    over(4, 6, ring_z.step)
    own_out.wait()
    ring_o.begin()
    over(6, 7, ring_z.step)
    ring_z.arrive()
    own_z = project(1, wz, outz, rz, lambda j: None)
    own_x.wait()
    over(1, N, lambda k: slab_to(0, k).wait())
    wait_all(keys_to)

    left = left_lanes(TOK)
    left1 = left_lanes(1)
    eye = onehot(iota((TOK, TOK), 0) == iota((TOK, TOK), 1))

    def gathered(ref, s8, h):
        o = pl.multiple_of(s8 * 32, 32)
        so = pl.multiple_of(256 + (s8 // 4) * 16, 16)
        parts = []
        for e in range(8):
            parts.append(ref[2 * e + h, pl.ds(o, 32), :])
            parts.append(ref[2 * e + h, pl.ds(so, 16), :])
        return jnp.concatenate(parts, axis=0)

    def back_in_order(ref, s8, p2):
        a0 = mm(p2, gathered(ref, s8, 0))
        a1 = mm(p2, gathered(ref, s8, 1))
        low = jnp.where(left, a0[:TOK], turn(a1[:TOK]))
        high = jnp.where(left, turn(a0[TOK:]), a1[TOK:])
        return low, high

    def places(s):
        cols = lax.dot_general(eye, aux[s], NT, preferred_element_type=F32).astype(jnp.int32)
        e_col, p_col = cols[:, 3:4], cols[:, 4:5]
        target = e_col * 48 + jnp.where(p_col < 32, p_col, p_col + lax.rem(s, 4) * 4)
        return onehot(iota((TOK, 384), 1) == target)

    def unpermute(s8):
        ps[s8, :TOK, :] = places(s8)
        ps[s8, TOK:, :] = places(s8 + 8)
        low, high = back_in_order(rx, s8, ps[s8])
        xs[pl.ds(pl.multiple_of(8 + s8 * TOK, 8), TOK), :] = low
        xs[pl.ds(pl.multiple_of(8 + (s8 + 8) * TOK, 8), TOK), :] = high

    unpermute(7)
    edge_out[...] = xs[3064:3080, :].astype(BF16)
    edge = pltpu.make_async_remote_copy(
        edge_out, edge_in, es.at[0], es.at[1],
        device_id=(lax.rem(c + 1, N), me), device_id_type=MESH)

    def unp(s8, _):
        unpermute(s8)
        return 0

    edge.start()
    lax.fori_loop(0, 7, unp, 0)
    over(0, 1, ring_o.step)
    edge.wait()
    first = jnp.where(c == 0, 0.0, 1.0)
    xs[0:8, :] = edge_in[...].astype(F32)[8:] * first

    state[...] = jnp.zeros((128, 128), F32)
    pre[...] = jnp.zeros((8, 128), F32)
    r2, c2 = iota((384, TOK), 0), iota((384, TOK), 1)
    low_eye = jnp.where(((r2 < TOK) & (c2 <= r2)) | (c2 == r2 - TOK), 1.0, 0.0)
    upper = jnp.where(iota((TOK, TOK), 0) <= iota((TOK, TOK), 1), 1.0, 0.0)

    def states(s, _):
        a = aux[s].astype(F32)
        rows = []
        for h in range(2):
            v = a[h : h + 1] + bias[h]
            rows.append(jnp.maximum(v, 0.0) + jnp.log1p(jnp.exp(-jnp.abs(v))))
        logs = [-(rate[h] * rows[h] + a[2:3]) for h in range(2)]
        rows8 = jnp.concatenate(logs + rows + [jnp.zeros((4, TOK), F32)], axis=0)
        colf = lax.dot_general(low_eye, rows8, NT, precision=HIGHEST, preferred_element_type=F32)
        climb = jnp.dot(rows8, upper, precision=HIGHEST, preferred_element_type=F32)
        clr[s] = climb
        cl = jnp.where(left, colf[:TOK, 0:1], colf[:TOK, 1:2])
        dts = jnp.where(left, colf[TOK:, 2:3], colf[TOK:, 3:4])
        cls[s] = cl
        tot = jnp.where(left1, climb[0:1, TOK - 1 : TOK], climb[1:2, TOK - 1 : TOK])
        full = xs[pl.ds(pl.multiple_of(s * TOK, 8), TOK + 8), :]
        w = conv[3:4, :] * full[8:]
        for k in range(3):
            w = w + conv[k : k + 1, :] * pltpu.roll(full, 3 - k, 0)[8:]
        u = w / (1.0 + jnp.exp(-w))
        us[s] = u
        dtu = dts * u
        dtus[s] = dtu.astype(BF16)
        weighted = (jnp.exp(tot - cl) * dtu).astype(BF16)
        old = state[...]
        ents[s] = old.astype(BF16)
        keys = bb[s]
        state[...] = jnp.exp(tot) * old + lax.dot_general(
            keys, weighted, TN, preferred_element_type=F32
        )
        before = pre[...]
        ys[s] = cl + before[0:1]
        pre[...] = before + tot

        @pl.when(lax.rem(s, 5) == 4)
        def _():
            ring_o.step(1 + s // 5)

        return 0

    lax.fori_loop(0, N, states, 0)
    fin_out[0:128, :] = state[...].astype(BF16)
    tot = pre[0:1]
    t1 = tot.astype(BF16)
    t2 = (tot - t1.astype(F32)).astype(BF16)
    t3 = (tot - t1.astype(F32) - t2.astype(F32)).astype(BF16)
    fin_out[128:144, :] = jnp.concatenate([t1, t2, t3, jnp.zeros((13, 128), BF16)], axis=0)

    def final_to(k):
        return pltpu.make_async_remote_copy(
            fin_out, fins.at[c], fs.at[k], fr.at[k],
            device_id=(lax.rem(c + k, N), me), device_id_type=MESH)

    def give(k, _):
        final_to(k).start()
        return 0

    lax.fori_loop(1, N - c, give, 0)
    mask = iota((TOK, TOK), 0) >= iota((TOK, TOK), 1)
    over(1, N, lambda k: queries_to(k).wait_recv())

    def inside(s, _):
        queries = bcq[s]
        gram = lax.dot_general(queries, bb[s], NT, preferred_element_type=F32)
        cl = cls[s]
        cr = clr[s]
        dtu = dtus[s]
        halves = []
        for h in range(2):
            d = cl[:, 64 * h : 64 * h + 1] - cr[h : h + 1]
            m = jnp.exp(jnp.where(mask, d, -1e30)) * gram
            halves.append(mm(m.astype(BF16), dtu))
        inter = mm(queries, ents[s]) * jnp.exp(cl)
        skip = jnp.where(left1, dskip[0], dskip[1])
        us[s] = jnp.where(left, halves[0], halves[1]) + inter + skip * us[s]

        @pl.when(lax.rem(s, 5) == 4)
        def _():
            ring_o.step(4 + s // 5)

        return 0

    lax.fori_loop(0, N, inside, 0)

    def gave(k, _):
        final_to(k).wait_send()
        return 0

    lax.fori_loop(1, N - c, gave, 0)
    state[...] = jnp.zeros((128, 128), F32)

    def arrive(k, _):
        final_to(k).wait_recv()
        return 0

    lax.fori_loop(1, c + 1, arrive, 0)

    def lap(i, _):
        f = fins[i].astype(F32)
        tot = f[128:129] + f[129:130] + f[130:131]
        state[...] = jnp.exp(tot) * state[...] + f[:128]
        return 0

    lax.fori_loop(0, c, lap, 0)
    incoming = state[...].astype(BF16)
    rb, cb = iota((128, 128), 0), iota((128, 128), 1)
    means = jnp.where(rb // 64 == cb // 64, 1.0 / 64, 0.0)

    def stage(j, k):
        g = lax.rem(me + k, N)
        span = pl.ds(0, 128) if j == 0 else pl.ds(128, 160)
        return pltpu.make_async_remote_copy(
            out.at[g, span, :], back.at[me, span, :], ks.at[j, k], kr.at[j, k],
            device_id=(c, g), device_id_type=MESH)

    def launch(j):
        def one(k, _):
            stage(j, k).start()
            return 0
        lax.fori_loop(1, N, one, 0)

    def finish(s, z):
        y = us[s] + jnp.exp(ys[s]) * mm(bcq[s], incoming)
        v = y * (z / (1.0 + jnp.exp(-z)))
        ms = jnp.dot(v * v, means, precision=HIGHEST, preferred_element_type=F32)
        normed = (v * lax.rsqrt(ms + 1e-5) * gain[...]).astype(BF16)
        a = aux[s].astype(F32).astype(jnp.int32)
        e_row, p_row = a[3:4], a[4:5]
        target = e_row * 48 + jnp.where(p_row < 32, p_row, p_row + lax.rem(s, 4) * 4)
        return mm(onehot(iota((384, TOK), 0) == target), normed)

    left384 = left_lanes(384)

    def closing(s8, _):
        zl, zh = back_in_order(rz, s8, ps[s8])
        tl = finish(s8, zl)
        th = finish(s8 + 8, zh)
        for h in range(2):
            v = jnp.where(left384, tl, turn(th)) if h == 0 else jnp.where(left384, turn(tl), th)
            fresh = lax.rem(s8, 4) == 0
            total = jnp.where(fresh, 0.0, acc[h]) + v
            acc[h] = total
            for e in range(8):
                out[2 * e + h, pl.ds(pl.multiple_of(s8 * 32, 32), 32), :] = v[
                    e * 48 : e * 48 + 32
                ].astype(BF16)
                out[2 * e + h, pl.ds(pl.multiple_of(256 + (s8 // 4) * 16, 16), 16), :] = total[
                    e * 48 + 32 : e * 48 + 48
                ].astype(BF16)
        return 0

    acc[...] = jnp.zeros((2, 384, 128), F32)
    own_z.wait()
    over(1, N, lambda k: slab_to(1, k).wait_recv())
    lax.fori_loop(0, 4, closing, 0)
    launch(0)
    lax.fori_loop(4, 8, closing, 0)
    launch(1)
    own_back = pltpu.make_async_copy(out.at[me], back.at[me], ls.at[8])
    own_back.start()


    def big_to(part, q, k):
        cols = pl.ds(pl.multiple_of(q * 512, 512), 512)
        return pltpu.make_async_remote_copy(
            o.at[pl.ds(rows_of(peer(k)), 32), cols], big.at[me, :, cols],
            qs.at[q, k], qr.at[q, k], **to(k))

    def small_to(k):
        return pltpu.make_async_remote_copy(
            osm.at[peer(k)], rsmall.at[me], qs.at[4, k], qr.at[4, k], **to(k))

    ring_o.arrive()
    own_back.wait()
    over(1, N, lambda k: stage(0, k).wait())
    over(1, N, lambda k: stage(1, k).wait())
    for j in range(8):
        even = back[2 * j].astype(F32)
        odd = back[2 * j + 1].astype(F32)
        a[:288, 128 * j : 128 * j + 128] = jnp.where(left288, even, turn(odd)).astype(BF16)
        a[288:, 128 * j : 128 * j + 128] = jnp.where(left288, turn(even), odd).astype(BF16)
    r256b, c64 = iota((256, 64), 0), iota((256, 64), 1)

    def quarter(q, total):
        for i in range(2):
            t = mm(a[...], jnp.concatenate([wo[4 * q + 2 * i], wo[4 * q + 2 * i + 1]], axis=1))
            o[:, pl.ds(pl.multiple_of(q * 512 + i * 256, 256), 256)] = t.astype(BF16)
        over(1, N, lambda k: big_to(0, q, k).start())
        cols = pl.ds(pl.multiple_of(q * 512, 512), 512)
        rows = jnp.concatenate([o[256:288, cols], o[544:576, cols]], axis=0)
        place = onehot(
            (lax.rem(r256b // 4, 4) == q) & (c64 == (r256b // 16) * 4 + lax.rem(r256b, 4))
        )
        return total + mm(place, rows)

    total = lax.fori_loop(0, 4, quarter, jnp.zeros((256, 512), F32))
    osm[...] = total.astype(BF16).reshape(16, 16, 512)
    over(1, N, lambda k: small_to(k).start())
    own = [
        pltpu.make_async_copy(o.at[pl.ds(rows_of(me), 32), :], big.at[me], ls.at[9]),
        pltpu.make_async_copy(osm.at[me], rsmall.at[me], ls.at[10]),
    ]
    for cp in own:
        cp.start()
    mine = lax.dot_general(
        eye, jnp.concatenate([e_row, p_row] + [jnp.zeros_like(e_row)] * 6, axis=0).astype(BF16),
        NT, preferred_element_type=F32,
    ).astype(jnp.int32)
    e_col, p_col = mine[:, 0:1], mine[:, 1:2]
    c512 = iota((TOK, 512), 1)
    pick = onehot((c512 // 64 == e_col) & (lax.rem(c512, 32) == p_col))
    c256b = iota((TOK, 256), 1)
    for ring in rings:
        ring.sent()
    over(1, N, lambda k: queries_to(k).wait_send())
    over(1, N, lambda k: slab_to(1, k).wait_send())
    for cp in own:
        cp.wait()
    for q in range(4):
        over(1, N, lambda k: big_to(0, q, k).wait())
        cols = slice(q * 512, q * 512 + 512)
        res[:, cols] = mm(pick, big[:, :, cols].reshape(512, 512)).astype(BF16)
    over(1, N, lambda k: small_to(k).wait())
    late = rsmall[...].reshape(256, 512)
    for q in range(4):
        pickq = onehot(
            (c256b // 32 == e_col) & (lax.rem(c256b, 16) == q * 4 + p_col - 32) & (p_col >= 32)
        )
        cols = slice(q * 512, q * 512 + 512)
        res[:, cols] = (res[:, cols].astype(F32) + mm(pickq, late)).astype(BF16)


VM = pl.BlockSpec(memory_space=pltpu.VMEM)
SM = pl.BlockSpec(memory_space=pltpu.SMEM)
DMA = pltpu.SemaphoreType.DMA


def on_device(
    tokens, expert_ids, damping, in_weight, out_weight, w_bc, w_dt, rate, dt_bias, d_skip,
    gain, conv_weight,
):
    def v(*dims, dtype=BF16):
        return pltpu.VMEM(dims, dtype)

    return pl.pallas_call(
        layer_kernel,
        name="layer",
        out_shape=jax.ShapeDtypeStruct((TOK, WIDTH), BF16),
        in_specs=[VM] * 7 + [SM] * 3 + [VM] * 2,
        out_specs=VM,
        scratch_shapes=[
            v(N, 128, 1024), v(N, 128, 1024), v(N, 1024, 128), v(576, WIDTH),
            v(8, 32, WIDTH), v(8, 16, 512), v(TOK, 128), v(TOK, 128), v(N, 16, TOK),
            v(N, 16, 512), v(N, TOK, 128), v(N, TOK, 128), v(N, 16, TOK),
            v(N, 288, 128), v(N, 288, 128), v(N, 288, 128), v(N, 288, 128),
            v(3080, 128, dtype=F32), v(8, 384, 384), v(N, TOK, 128, dtype=F32), v(N, TOK, 128),
            v(N, TOK, 128, dtype=F32), v(N, 8, TOK, dtype=F32), v(N, 128, 128),
            v(N, TOK, 128, dtype=F32), v(8, 128, dtype=F32), v(128, 128, dtype=F32),
            v(16, 128), v(16, 128), v(144, 128), v(N, 144, 128), v(2, 384, 128, dtype=F32),
            v(N, 288, 128), v(N, 288, 128), v(576, 1024), v(576, WIDTH), v(N, 16, 512),
            v(N, 32, WIDTH), v(N, 16, 512),
            DMA((3, 32)), DMA((3, 32)), DMA((5, N)), DMA((5, N)), DMA((2, N)), DMA((2, N)),
            DMA((2,)), DMA((N,)), DMA((N,)), DMA((2, N)), DMA((2, N)),
            DMA((5, N)), DMA((5, N)), DMA((11,)),
        ],
        compiler_params=pltpu.CompilerParams(
            collective_id=0, has_side_effects=True, vmem_limit_bytes=VLIM
        ),
    )(
        tokens, expert_ids.reshape(1, TOK), damping.reshape(1, TOK),
        in_weight.reshape(256, 1024), out_weight[0], w_bc, w_dt, rate, dt_bias, d_skip,
        gain.reshape(1, 128), conv_weight,
    )


def solution(mesh):
    placed = (
        P(("ctx", "exp"), None), P(("ctx", "exp"), None), P(("ctx", "exp")),
        P("exp", "ctx", None, None), P("exp", None, "ctx"), P(), P(),
        P("exp"), P("exp"), P("exp"), P("exp"), P(None, "exp"),
    )
    return jax.shard_map(
        on_device, mesh=mesh, in_specs=placed, out_specs=P(("ctx", "exp"), None), check_vma=False
    )
```

```python
import functools

import jax
import jax.numpy as jnp
from jax import lax
from jax.experimental import pallas as pl
from jax.experimental.pallas import tpu as pltpu
from jax.sharding import PartitionSpec as P

MESH = pl.DeviceIdType.MESH
F32 = jnp.float32
BF16 = jnp.bfloat16
HIGHEST = lax.Precision.HIGHEST
N = 16
TOK = 192
WIDTH = 2048
VLIM = 62 * 1024 * 1024
ORDER = (1, 4, 3, 12, 5, 15, 7, 13, 2, 8, 6, 9, 14, 11, 10)
NT = (((1,), (1,)), ((), ()))
TN = (((0,), (0,)), ((), ()))


def iota(shape, dim):
    return lax.broadcasted_iota(jnp.int32, shape, dim)


def onehot(cond):
    return jnp.where(cond, 1.0, 0.0).astype(BF16)


def mm(a, b):
    return jnp.dot(a, b, preferred_element_type=F32)


def left_lanes(rows):
    return iota((rows, 128), 1) < 64


def turn(x):
    return pltpu.roll(x, 64, 1)


def rows_of(src):
    return pl.multiple_of((src // 8) * 288 + lax.rem(src, 8) * 32, 32)


def over(first, last, do):
    def one(k, _):
        do(k)
        return 0

    lax.fori_loop(first, last, one, 0)


class Ring:
    def __init__(self, me, c, view, ss, rs):
        self.me, self.c, self.view, self.ss, self.rs = me, c, view, ss, rs
        self.z, self.core = c // 2, lax.rem(c, 2)

    def piece(self, up, i, core):
        far = i // 2
        chip = lax.rem(self.z - far + 8, 8) if up else lax.rem(self.z + far, 8)
        half = lax.rem(i, 2) if up else lax.rem(i + 1, 2)
        return self.view(2 * chip + core, half)

    def copy(self, ref, sem, to):
        return pltpu.make_async_remote_copy(
            ref, ref, self.ss.at[sem], self.rs.at[sem],
            device_id=(to, self.me), device_id_type=MESH)

    def along(self, up, i):
        to = lax.rem(self.c + 2, N) if up else lax.rem(self.c + N - 2, N)
        return self.copy(self.piece(up, i, self.core), i if up else 7 + i, to)

    def landing(self, up, i):
        ref = self.piece(up, i + 2, self.core)
        return self.copy(ref, i if up else 7 + i, self.c + 1 - 2 * self.core)

    def across(self, up, i, core):
        sem = 14 + i if up else 23 + i
        return self.copy(self.piece(up, i, core), sem, self.c + 1 - 2 * self.core)

    def begin(self):
        def one(i):
            self.along(True, i).start()
            self.along(False, i).start()
            self.across(True, i, self.core).start()

        over(0, 2, one)

    def step(self, i):
        for up in (True, False):
            self.landing(up, i).wait_recv()

            @pl.when(i < 5)
            def _():
                self.along(up, i + 2).start()

            self.across(up, i + 2, self.core).start()

    def arrive(self):
        over(0, 9, lambda i: self.across(True, i, 1 - self.core).wait_recv())
        over(2, 9, lambda i: self.across(False, i, 1 - self.core).wait_recv())

    def sent(self):
        for up in (True, False):
            over(0, 7, lambda i: self.along(up, i).wait_send())
        over(0, 9, lambda i: self.across(True, i, self.core).wait_send())
        over(2, 9, lambda i: self.across(False, i, self.core).wait_send())


def layer_kernel(
    tok_any, ids, damp, w_in_any, w_own, w_bc_any, w_dt_any, rate, bias, dskip, gain, conv, res,
    wx, wz, wo, slots, sbig, ssmall, sb, sc, saux, small, bb, bcq, aux,
    outx, outz, rx, rz,
    xs, ps, us, dtus, cls, clr, ents, ys, pre, state, edge_out, edge_in,
    fin_out, fins, acc, out, back, a, o, osm, big, rsmall,
    tok, w_in, w_bc, w_dt, ring_s, ring_r, ds, dr, ps_, pr_, es, fs, fr, ks, kr, qs, qr, ls,
):
    me = lax.axis_index("exp")
    c = lax.axis_index("ctx")
    bar = pltpu.get_barrier_semaphore()

    def greet(k):
        pl.semaphore_signal(bar, inc=1, device_id=(c, lax.rem(me + k, N)), device_id_type=MESH)
        pl.semaphore_signal(bar, inc=1, device_id=(lax.rem(c + k, N), me), device_id_type=MESH)

    over(1, N, greet)
    own_out = pltpu.make_async_copy(w_own, wo.at[c], ls.at[0])
    loads = [
        pltpu.make_async_copy(src, dst, ls.at[11 + i])
        for i, (src, dst) in enumerate([(w_in_any, w_in), (tok_any, tok), (w_bc_any, w_bc), (w_dt_any, w_dt)])
    ]
    for cp in loads:
        cp.start()
    own_out.start()

    def rows_view(ref, size):
        def view(shard, half):
            return ref.at[shard, pl.ds(pl.multiple_of(half * size, size), size), :]
        return view

    rings = [
        Ring(me, c, rows_view(ref, size), ring_s.at[i], ring_r.at[i])
        for i, (ref, size) in enumerate([(wx, 64), (wz, 64), (wo, 512)])
    ]
    ring_x, ring_z, ring_o = rings
    r, q2 = iota((128, 256), 0), iota((128, 256), 1)
    loads[0].wait()
    wx[c] = mm(onehot(q2 == 2 * r), w_in[...]).astype(BF16)
    loads[1].wait()

    e_row = ids[...]
    oh = onehot(iota((8, TOK), 0) == e_row)
    earlier = onehot(iota((TOK, TOK), 0) < iota((TOK, TOK), 1))
    before = mm(oh, earlier)
    p_row = jnp.sum(before * oh.astype(F32), axis=0, keepdims=True).astype(jnp.int32)
    pick_big = onehot(iota((256, TOK), 0) == jnp.where(p_row < 32, e_row * 32 + p_row, -1))
    r128 = iota((128, TOK), 0)
    smallhit = (r128 // 16 == e_row) & (lax.rem(r128, 4) == p_row - 32)
    q128 = lax.rem(r128 // 4, 4)
    smalls = jnp.zeros((128, 512), F32)
    for q in range(4):
        cols = slice(q * 512, q * 512 + 512)
        t = tok[:, cols]
        sbig[:, :, cols] = mm(pick_big, t).astype(BF16).reshape(8, 32, 512)
        smalls = smalls + mm(onehot(smallhit & (q128 == q)), t)
    ssmall[...] = smalls.astype(BF16).reshape(8, 16, 512)

    wz[c] = mm(onehot(q2 == 2 * r + 1), w_in[...]).astype(BF16)
    loads[2].wait()
    loads[3].wait()
    shared = mm(tok[...], w_bc[...]).astype(BF16)
    sb[...] = shared[:, :128]
    sc[...] = shared[:, 128:]
    dt = lax.dot_general(w_dt[...], tok[...], NT, preferred_element_type=F32).astype(BF16)
    extra = jnp.concatenate(
        [dt, damp[...], e_row.astype(BF16), p_row.astype(BF16), jnp.zeros((13, TOK), BF16)], axis=0
    )
    r256, c48 = iota((256, 48), 0), iota((256, 48), 1)
    kind = lax.rem(r256, 16)
    wanted = jnp.where(kind < 2, 2 * (r256 // 16) + kind, jnp.where(kind < 5, 30 + kind, 48))
    saux[...] = mm(onehot(c48 == wanted), extra).astype(BF16).reshape(16, 16, TOK)

    def peer(k):
        return lax.rem(me // 4 + k // 4, 4) * 4 + lax.rem(me + k % 4, 4)

    def to(k):
        return {"device_id": (c, peer(k)), "device_id_type": MESH}

    def slots_to(k):
        g = peer(k)
        return (
            pltpu.make_async_remote_copy(
                sbig.at[g // 2], slots.at[pl.ds(rows_of(me), 32), :],
                ds.at[0, k], dr.at[0, k], **to(k)),
            pltpu.make_async_remote_copy(
                ssmall.at[g // 2], small.at[me], ds.at[1, k], dr.at[1, k], **to(k)),
        )

    def keys_to(k):
        return (
            pltpu.make_async_remote_copy(sb, bb.at[me], ds.at[2, k], dr.at[2, k], **to(k)),
            pltpu.make_async_remote_copy(
                saux.at[peer(k)], aux.at[me], ds.at[3, k], dr.at[3, k], **to(k)),
        )

    def queries_to(k):
        return (pltpu.make_async_remote_copy(sc, bcq.at[me], ds.at[4, k], dr.at[4, k], **to(k)),)

    def start_all(make, some=ORDER):
        for k in some:
            for cp in make(k):
                cp.start()

    def wait_all(make):
        def one(k):
            for cp in make(k):
                cp.wait()
        over(1, N, one)

    pl.semaphore_wait(bar, 2 * (N - 1))
    ring_x.begin()
    start_all(slots_to, ORDER[:4])
    own = [
        pltpu.make_async_copy(sbig.at[me // 2], slots.at[pl.ds(rows_of(me), 32), :], ls.at[1]),
        pltpu.make_async_copy(ssmall.at[me // 2], small.at[me], ls.at[2]),
        pltpu.make_async_copy(sb, bb.at[me], ls.at[3]),
        pltpu.make_async_copy(sc, bcq.at[me], ls.at[4]),
        pltpu.make_async_copy(saux.at[me], aux.at[me], ls.at[5]),
    ]
    for cp in own:
        cp.start()
    over(0, 1, ring_x.step)
    start_all(slots_to, ORDER[4:8])
    over(1, 3, ring_x.step)
    start_all(slots_to, ORDER[8:12])
    over(3, 5, ring_x.step)
    ring_z.begin()
    start_all(slots_to, ORDER[12:])
    over(5, 7, ring_x.step)
    start_all(keys_to)
    ring_x.arrive()
    over(0, 2, ring_z.step)
    for cp in own:
        cp.wait()
    wait_all(slots_to)
    r64, c256 = iota((64, 256), 0), iota((64, 256), 1)
    flat = small[...].reshape(256, 512)
    for q in range(4):
        pickq = onehot(c256 == (r64 // 4) * 16 + q * 4 + lax.rem(r64, 4))
        rows = mm(pickq, flat).astype(BF16)
        slots[256:288, q * 512 : q * 512 + 512] = rows[:32]
        slots[544:576, q * 512 : q * 512 + 512] = rows[32:]

    left288 = left_lanes(288)

    def slab_to(part, k):
        src, dst = (outx, rx) if part == 0 else (outz, rz)
        span = (pl.ds(0, 288), pl.ds(128, 160), pl.ds(0, 128))[part]
        return pltpu.make_async_remote_copy(
            src.at[peer(k), span, :], dst.at[me, span, :], ps_.at[part, k], pr_.at[part, k],
            **to(k))

    def project(half, w, slab, got, between):
        def send(quad):
            for i in range(4):
                k = lax.rem(quad - me // 4 + 4, 4) * 4 + lax.rem(i - lax.rem(me, 4) + 4, 4)

                @pl.when(k != 0)
                def _():
                    slab_to(half, k).start()

        def at(j):
            return lax.rem(2 * j + 1 - j // 2 + me // 4, 4)

        def tile(j):
            quad = at(j)
            cols = pl.ds(pl.multiple_of(quad * 256, 256), 256)
            t2 = mm(slots[...], w[:, :, cols].reshape(WIDTH, 256))
            for i in range(2):
                t = t2[:288, 128 * i : 128 * i + 128]
                b = t2[288:, 128 * i : 128 * i + 128]
                slab[4 * quad + 2 * i] = jnp.where(left288, t, turn(b)).astype(BF16)
                slab[4 * quad + 2 * i + 1] = jnp.where(left288, turn(t), b).astype(BF16)

            @pl.when(j > 0)
            def _():
                send(at(j - 1))

            between(j)

        over(0, 4, tile)
        send(at(3))
        cp = pltpu.make_async_copy(slab.at[me], got.at[me], ls.at[6 + half])
        cp.start()
        return cp

    def ring_between(j):
        @pl.when(lax.rem(j, 2) == 1)
        def _():
            ring_z.step(2 + j // 2)

    own_x = project(0, wx, outx, rx, ring_between)
    start_all(queries_to)
    over(4, 6, ring_z.step)
    own_out.wait()
    ring_o.begin()
    over(6, 7, ring_z.step)
    ring_z.arrive()
    own_z = project(1, wz, outz, rz, lambda j: None)
    for k in ORDER:
        slab_to(2, k).start()
    own_x.wait()
    over(1, N, lambda k: slab_to(0, k).wait())
    wait_all(keys_to)

    left = left_lanes(TOK)
    left1 = left_lanes(1)
    eye = onehot(iota((TOK, TOK), 0) == iota((TOK, TOK), 1))

    def gathered(ref, s8, h):
        o = pl.multiple_of(s8 * 32, 32)
        so = pl.multiple_of(256 + (s8 // 4) * 16, 16)
        parts = []
        for e in range(8):
            parts.append(ref[2 * e + h, pl.ds(o, 32), :])
            parts.append(ref[2 * e + h, pl.ds(so, 16), :])
        return jnp.concatenate(parts, axis=0)

    def back_in_order(ref, s8, p2):
        a0 = mm(p2, gathered(ref, s8, 0))
        a1 = mm(p2, gathered(ref, s8, 1))
        low = jnp.where(left, a0[:TOK], turn(a1[:TOK]))
        high = jnp.where(left, turn(a0[TOK:]), a1[TOK:])
        return low, high

    def places(s):
        cols = lax.dot_general(eye, aux[s], NT, preferred_element_type=F32).astype(jnp.int32)
        e_col, p_col = cols[:, 3:4], cols[:, 4:5]
        target = e_col * 48 + jnp.where(p_col < 32, p_col, p_col + lax.rem(s, 4) * 4)
        return onehot(iota((TOK, 384), 1) == target)

    def unpermute(s8):
        ps[s8, :TOK, :] = places(s8)
        ps[s8, TOK:, :] = places(s8 + 8)
        low, high = back_in_order(rx, s8, ps[s8])
        xs[pl.ds(pl.multiple_of(8 + s8 * TOK, 8), TOK), :] = low
        xs[pl.ds(pl.multiple_of(8 + (s8 + 8) * TOK, 8), TOK), :] = high

    unpermute(7)
    edge_out[...] = xs[3064:3080, :].astype(BF16)
    edge = pltpu.make_async_remote_copy(
        edge_out, edge_in, es.at[0], es.at[1],
        device_id=(lax.rem(c + 1, N), me), device_id_type=MESH)

    def unp(s8, _):
        unpermute(s8)
        return 0

    edge.start()
    lax.fori_loop(0, 7, unp, 0)
    over(0, 1, ring_o.step)
    edge.wait()
    first = jnp.where(c == 0, 0.0, 1.0)
    xs[0:8, :] = edge_in[...].astype(F32)[8:] * first

    state[...] = jnp.zeros((128, 128), F32)
    pre[...] = jnp.zeros((8, 128), F32)
    r2, c2 = iota((384, TOK), 0), iota((384, TOK), 1)
    low_eye = jnp.where(((r2 < TOK) & (c2 <= r2)) | (c2 == r2 - TOK), 1.0, 0.0)
    upper = jnp.where(iota((TOK, TOK), 0) <= iota((TOK, TOK), 1), 1.0, 0.0)

    def states(s, _):
        a = aux[s].astype(F32)
        rows = []
        for h in range(2):
            v = a[h : h + 1] + bias[h]
            rows.append(jnp.maximum(v, 0.0) + jnp.log1p(jnp.exp(-jnp.abs(v))))
        logs = [-(rate[h] * rows[h] + a[2:3]) for h in range(2)]
        rows8 = jnp.concatenate(logs + rows + [jnp.zeros((4, TOK), F32)], axis=0)
        colf = lax.dot_general(low_eye, rows8, NT, precision=HIGHEST, preferred_element_type=F32)
        climb = jnp.dot(rows8, upper, precision=HIGHEST, preferred_element_type=F32)
        clr[s] = climb
        cl = jnp.where(left, colf[:TOK, 0:1], colf[:TOK, 1:2])
        dts = jnp.where(left, colf[TOK:, 2:3], colf[TOK:, 3:4])
        cls[s] = cl
        tot = jnp.where(left1, climb[0:1, TOK - 1 : TOK], climb[1:2, TOK - 1 : TOK])
        full = xs[pl.ds(pl.multiple_of(s * TOK, 8), TOK + 8), :]
        w = conv[3:4, :] * full[8:]
        for k in range(3):
            w = w + conv[k : k + 1, :] * pltpu.roll(full, 3 - k, 0)[8:]
        u = w / (1.0 + jnp.exp(-w))
        us[s] = u
        dtu = dts * u
        dtus[s] = dtu.astype(BF16)
        weighted = (jnp.exp(tot - cl) * dtu).astype(BF16)
        old = state[...]
        ents[s] = old.astype(BF16)
        keys = bb[s]
        state[...] = jnp.exp(tot) * old + lax.dot_general(
            keys, weighted, TN, preferred_element_type=F32
        )
        before = pre[...]
        ys[s] = cl + before[0:1]
        pre[...] = before + tot

        @pl.when(lax.rem(s, 5) == 4)
        def _():
            ring_o.step(1 + s // 5)

        return 0

    lax.fori_loop(0, N, states, 0)
    fin_out[0:128, :] = state[...].astype(BF16)
    tot = pre[0:1]
    t1 = tot.astype(BF16)
    t2 = (tot - t1.astype(F32)).astype(BF16)
    t3 = (tot - t1.astype(F32) - t2.astype(F32)).astype(BF16)
    fin_out[128:144, :] = jnp.concatenate([t1, t2, t3, jnp.zeros((13, 128), BF16)], axis=0)

    def final_to(k):
        return pltpu.make_async_remote_copy(
            fin_out, fins.at[c], fs.at[k], fr.at[k],
            device_id=(lax.rem(c + k, N), me), device_id_type=MESH)

    def give(k, _):
        final_to(k).start()
        return 0

    lax.fori_loop(1, N - c, give, 0)
    mask = iota((TOK, TOK), 0) >= iota((TOK, TOK), 1)
    over(1, N, lambda k: queries_to(k)[0].wait_recv())

    def inside(s, _):
        queries = bcq[s]
        gram = lax.dot_general(queries, bb[s], NT, preferred_element_type=F32)
        cl = cls[s]
        cr = clr[s]
        dtu = dtus[s]
        halves = []
        for h in range(2):
            d = cl[:, 64 * h : 64 * h + 1] - cr[h : h + 1]
            m = jnp.exp(jnp.where(mask, d, -1e30)) * gram
            halves.append(mm(m.astype(BF16), dtu))
        inter = mm(queries, ents[s]) * jnp.exp(cl)
        skip = jnp.where(left1, dskip[0], dskip[1])
        us[s] = jnp.where(left, halves[0], halves[1]) + inter + skip * us[s]

        @pl.when(lax.rem(s, 5) == 4)
        def _():
            ring_o.step(4 + s // 5)

        return 0

    lax.fori_loop(0, N, inside, 0)

    def gave(k, _):
        final_to(k).wait_send()
        return 0

    lax.fori_loop(1, N - c, gave, 0)
    state[...] = jnp.zeros((128, 128), F32)

    def arrive(k, _):
        final_to(k).wait_recv()
        return 0

    lax.fori_loop(1, c + 1, arrive, 0)

    def lap(i, _):
        f = fins[i].astype(F32)
        tot = f[128:129] + f[129:130] + f[130:131]
        state[...] = jnp.exp(tot) * state[...] + f[:128]
        return 0

    lax.fori_loop(0, c, lap, 0)
    incoming = state[...].astype(BF16)
    rb, cb = iota((128, 128), 0), iota((128, 128), 1)
    means = jnp.where(rb // 64 == cb // 64, 1.0 / 64, 0.0)

    def stage(j, k):
        span = pl.ds(256, 32) if j == 4 else pl.ds(64 * j, 64)
        return pltpu.make_async_remote_copy(
            out.at[peer(k), span, :], back.at[me, span, :], ks.at[j, k], kr.at[j, k], **to(k))

    def launch(j):
        for k in ORDER:
            stage(j, k).start()

    def finish(s, z):
        y = us[s] + jnp.exp(ys[s]) * mm(bcq[s], incoming)
        v = y * (z / (1.0 + jnp.exp(-z)))
        ms = jnp.dot(v * v, means, precision=HIGHEST, preferred_element_type=F32)
        normed = (v * lax.rsqrt(ms + 1e-5) * gain[...]).astype(BF16)
        a = aux[s].astype(F32).astype(jnp.int32)
        e_row, p_row = a[3:4], a[4:5]
        target = e_row * 48 + jnp.where(p_row < 32, p_row, p_row + lax.rem(s, 4) * 4)
        return mm(onehot(iota((384, TOK), 0) == target), normed)

    left384 = left_lanes(384)

    def closing(s8, _):
        zl, zh = back_in_order(rz, s8, ps[s8])
        tl = finish(s8, zl)
        th = finish(s8 + 8, zh)
        for h in range(2):
            v = jnp.where(left384, tl, turn(th)) if h == 0 else jnp.where(left384, turn(tl), th)
            fresh = lax.rem(s8, 4) == 0
            total = jnp.where(fresh, 0.0, acc[h]) + v
            acc[h] = total
            for e in range(8):
                out[2 * e + h, pl.ds(pl.multiple_of(s8 * 32, 32), 32), :] = v[
                    e * 48 : e * 48 + 32
                ].astype(BF16)
                out[2 * e + h, pl.ds(pl.multiple_of(256 + (s8 // 4) * 16, 16), 16), :] = total[
                    e * 48 + 32 : e * 48 + 48
                ].astype(BF16)
        return 0

    acc[...] = jnp.zeros((2, 384, 128), F32)
    own_z.wait()
    over(1, N, lambda k: slab_to(1, k).wait_recv())
    lax.fori_loop(4, 6, closing, 0)
    launch(2)
    lax.fori_loop(6, 8, closing, 0)
    launch(3)
    over(1, N, lambda k: slab_to(2, k).wait_recv())
    lax.fori_loop(0, 2, closing, 0)
    launch(0)
    lax.fori_loop(2, 4, closing, 0)
    launch(1)
    launch(4)
    own_back = pltpu.make_async_copy(out.at[me], back.at[me], ls.at[8])
    own_back.start()


    def big_to(part, q, k):
        cols = pl.ds(pl.multiple_of(q * 512, 512), 512)
        return pltpu.make_async_remote_copy(
            o.at[pl.ds(rows_of(peer(k)), 32), cols], big.at[me, :, cols],
            qs.at[q, k], qr.at[q, k], **to(k))

    def small_to(k):
        return pltpu.make_async_remote_copy(
            osm.at[peer(k)], rsmall.at[me], qs.at[4, k], qr.at[4, k], **to(k))

    ring_o.arrive()
    own_back.wait()
    for j in (2, 3, 0, 1, 4):
        over(1, N, lambda k: stage(j, k).wait())
    for j in range(8):
        even = back[2 * j].astype(F32)
        odd = back[2 * j + 1].astype(F32)
        a[:288, 128 * j : 128 * j + 128] = jnp.where(left288, even, turn(odd)).astype(BF16)
        a[288:, 128 * j : 128 * j + 128] = jnp.where(left288, turn(even), odd).astype(BF16)
    r256b, c64 = iota((256, 64), 0), iota((256, 64), 1)

    def quarter(q, total):
        for i in range(2):
            t = mm(a[...], jnp.concatenate([wo[4 * q + 2 * i], wo[4 * q + 2 * i + 1]], axis=1))
            o[:, pl.ds(pl.multiple_of(q * 512 + i * 256, 256), 256)] = t.astype(BF16)
        for k in ORDER:
            big_to(0, q, k).start()
        cols = pl.ds(pl.multiple_of(q * 512, 512), 512)
        rows = jnp.concatenate([o[256:288, cols], o[544:576, cols]], axis=0)
        place = onehot(
            (lax.rem(r256b // 4, 4) == q) & (c64 == (r256b // 16) * 4 + lax.rem(r256b, 4))
        )
        return total + mm(place, rows)

    total = lax.fori_loop(0, 4, quarter, jnp.zeros((256, 512), F32))
    osm[...] = total.astype(BF16).reshape(16, 16, 512)
    for k in ORDER:
        small_to(k).start()
    own = [
        pltpu.make_async_copy(o.at[pl.ds(rows_of(me), 32), :], big.at[me], ls.at[9]),
        pltpu.make_async_copy(osm.at[me], rsmall.at[me], ls.at[10]),
    ]
    for cp in own:
        cp.start()
    mine = lax.dot_general(
        eye, jnp.concatenate([e_row, p_row] + [jnp.zeros_like(e_row)] * 6, axis=0).astype(BF16),
        NT, preferred_element_type=F32,
    ).astype(jnp.int32)
    e_col, p_col = mine[:, 0:1], mine[:, 1:2]
    c512 = iota((TOK, 512), 1)
    pick = onehot((c512 // 64 == e_col) & (lax.rem(c512, 32) == p_col))
    c256b = iota((TOK, 256), 1)
    for ring in rings:
        ring.sent()
    over(1, N, lambda k: queries_to(k)[0].wait_send())
    for part in (1, 2):
        over(1, N, lambda k: slab_to(part, k).wait_send())
    for cp in own:
        cp.wait()
    for q in range(4):
        over(1, N, lambda k: big_to(0, q, k).wait())
        cols = slice(q * 512, q * 512 + 512)
        res[:, cols] = mm(pick, big[:, :, cols].reshape(512, 512)).astype(BF16)
    over(1, N, lambda k: small_to(k).wait())
    late = rsmall[...].reshape(256, 512)
    for q in range(4):
        pickq = onehot(
            (c256b // 32 == e_col) & (lax.rem(c256b, 16) == q * 4 + p_col - 32) & (p_col >= 32)
        )
        cols = slice(q * 512, q * 512 + 512)
        res[:, cols] = (res[:, cols].astype(F32) + mm(pickq, late)).astype(BF16)


VM = pl.BlockSpec(memory_space=pltpu.VMEM)
SM = pl.BlockSpec(memory_space=pltpu.SMEM)
DMA = pltpu.SemaphoreType.DMA
ANY = pl.BlockSpec(memory_space=pl.ANY)


def on_device(
    tokens, expert_ids, damping, in_weight, out_weight, w_bc, w_dt, rate, dt_bias, d_skip,
    gain, conv_weight,
):
    def v(*dims, dtype=BF16):
        return pltpu.VMEM(dims, dtype)

    return pl.pallas_call(
        layer_kernel,
        name="layer",
        out_shape=jax.ShapeDtypeStruct((TOK, WIDTH), BF16),
        in_specs=[ANY, VM, VM] + [ANY] * 4 + [SM] * 3 + [VM] * 2,
        out_specs=VM,
        scratch_shapes=[
            v(N, 128, 1024), v(N, 128, 1024), v(N, 1024, 128), v(576, WIDTH),
            v(8, 32, WIDTH), v(8, 16, 512), v(TOK, 128), v(TOK, 128), v(N, 16, TOK),
            v(N, 16, 512), v(N, TOK, 128), v(N, TOK, 128), v(N, 16, TOK),
            v(N, 288, 128), v(N, 288, 128), v(N, 288, 128), v(N, 288, 128),
            v(3080, 128, dtype=F32), v(8, 384, 384), v(N, TOK, 128, dtype=F32), v(N, TOK, 128),
            v(N, TOK, 128, dtype=F32), v(N, 8, TOK, dtype=F32), v(N, 128, 128),
            v(N, TOK, 128, dtype=F32), v(8, 128, dtype=F32), v(128, 128, dtype=F32),
            v(16, 128), v(16, 128), v(144, 128), v(N, 144, 128), v(2, 384, 128, dtype=F32),
            v(N, 288, 128), v(N, 288, 128), v(576, 1024), v(576, WIDTH), v(N, 16, 512),
            v(N, 32, WIDTH), v(N, 16, 512),
            v(TOK, WIDTH), v(256, 1024), v(WIDTH, 256), v(32, WIDTH),
            DMA((3, 32)), DMA((3, 32)), DMA((5, N)), DMA((5, N)), DMA((3, N)), DMA((3, N)),
            DMA((2,)), DMA((N,)), DMA((N,)), DMA((5, N)), DMA((5, N)),
            DMA((5, N)), DMA((5, N)), DMA((15,)),
        ],
        compiler_params=pltpu.CompilerParams(
            collective_id=0, has_side_effects=True, vmem_limit_bytes=VLIM
        ),
    )(
        tokens, expert_ids.reshape(1, TOK), damping.reshape(1, TOK),
        in_weight.reshape(256, 1024), out_weight[0], w_bc, w_dt, rate, dt_bias, d_skip,
        gain.reshape(1, 128), conv_weight,
    )


def solution(mesh):
    placed = (
        P(("ctx", "exp"), None), P(("ctx", "exp"), None), P(("ctx", "exp")),
        P("exp", "ctx", None, None), P("exp", None, "ctx"), P(), P(),
        P("exp"), P("exp"), P("exp"), P("exp"), P(None, "exp"),
    )
    return jax.shard_map(
        on_device, mesh=mesh, in_specs=placed, out_specs=P(("ctx", "exp"), None), check_vma=False
    )
```

```python
import functools

import jax
import jax.numpy as jnp
from jax import lax
from jax.experimental import pallas as pl
from jax.experimental.pallas import tpu as pltpu
from jax.sharding import PartitionSpec as P

MESH = pl.DeviceIdType.MESH
F32 = jnp.float32
BF16 = jnp.bfloat16
HIGHEST = lax.Precision.HIGHEST
N = 16
TOK = 192
WIDTH = 2048
VLIM = 62 * 1024 * 1024
ORDER = (1, 4, 3, 12, 5, 15, 7, 13, 2, 8, 6, 9, 14, 11, 10)
NT = (((1,), (1,)), ((), ()))
TN = (((0,), (0,)), ((), ()))


def iota(shape, dim):
    return lax.broadcasted_iota(jnp.int32, shape, dim)


def onehot(cond):
    return jnp.where(cond, 1.0, 0.0).astype(BF16)


def mm(a, b):
    return jnp.dot(a, b, preferred_element_type=F32)


def left_lanes(rows):
    return iota((rows, 128), 1) < 64


def turn(x):
    return pltpu.roll(x, 64, 1)


def rows_of(src):
    return pl.multiple_of((src // 8) * 288 + lax.rem(src, 8) * 32, 32)


def over(first, last, do):
    def one(k, _):
        do(k)
        return 0

    lax.fori_loop(first, last, one, 0)


class Ring:
    def __init__(self, me, c, view, ss, rs):
        self.me, self.c, self.view, self.ss, self.rs = me, c, view, ss, rs
        self.z, self.core = c // 2, lax.rem(c, 2)

    def piece(self, up, i, core):
        far = i // 2
        chip = lax.rem(self.z - far + 8, 8) if up else lax.rem(self.z + far, 8)
        half = lax.rem(i, 2) if up else lax.rem(i + 1, 2)
        return self.view(2 * chip + core, half)

    def copy(self, ref, sem, to):
        return pltpu.make_async_remote_copy(
            ref, ref, self.ss.at[sem], self.rs.at[sem],
            device_id=(to, self.me), device_id_type=MESH)

    def along(self, up, i):
        to = lax.rem(self.c + 2, N) if up else lax.rem(self.c + N - 2, N)
        return self.copy(self.piece(up, i, self.core), i if up else 7 + i, to)

    def landing(self, up, i):
        ref = self.piece(up, i + 2, self.core)
        return self.copy(ref, i if up else 7 + i, self.c + 1 - 2 * self.core)

    def across(self, up, i, core):
        sem = 14 + i if up else 23 + i
        return self.copy(self.piece(up, i, core), sem, self.c + 1 - 2 * self.core)

    def begin(self):
        def one(i):
            self.along(True, i).start()
            self.along(False, i).start()
            self.across(True, i, self.core).start()

        over(0, 2, one)

    def step(self, i):
        for up in (True, False):
            self.landing(up, i).wait_recv()

            @pl.when(i < 5)
            def _():
                self.along(up, i + 2).start()

            self.across(up, i + 2, self.core).start()

    def arrive(self):
        over(0, 9, lambda i: self.across(True, i, 1 - self.core).wait_recv())
        over(2, 9, lambda i: self.across(False, i, 1 - self.core).wait_recv())

    def sent(self):
        for up in (True, False):
            over(0, 7, lambda i: self.along(up, i).wait_send())
        over(0, 9, lambda i: self.across(True, i, self.core).wait_send())
        over(2, 9, lambda i: self.across(False, i, self.core).wait_send())


def layer_kernel(
    tok_any, ids, damp, w_in_any, w_own, w_bc_any, w_dt_any, rate, bias, dskip, gain, conv, res,
    wx, wz, wo, slots, sbig, ssmall, sb, sc, saux, small, bb, bcq, aux,
    outx, outz, rx, rz,
    xs, ps, us, dtus, cls, clr, ents, ys, pre, state, edge_out, edge_in,
    fin_out, fin_in, chip_out, chips, half_out, half_in, acc, out, back, a, o, osm, big, rsmall,
    tok, w_in, w_bc, w_dt, ring_s, ring_r, ds, dr, ps_, pr_, es, fs, fr, ks, kr, qs, qr, ls,
):
    me = lax.axis_index("exp")
    c = lax.axis_index("ctx")
    bar = pltpu.get_barrier_semaphore()

    def greet(k):
        pl.semaphore_signal(bar, inc=1, device_id=(c, lax.rem(me + k, N)), device_id_type=MESH)
        pl.semaphore_signal(bar, inc=1, device_id=(lax.rem(c + k, N), me), device_id_type=MESH)

    over(1, N, greet)
    own_out = pltpu.make_async_copy(w_own, wo.at[c], ls.at[0])
    loads = [
        pltpu.make_async_copy(src, dst, ls.at[11 + i])
        for i, (src, dst) in enumerate([(w_in_any, w_in), (tok_any, tok), (w_bc_any, w_bc), (w_dt_any, w_dt)])
    ]
    for cp in loads:
        cp.start()
    own_out.start()

    def rows_view(ref, size):
        def view(shard, half):
            return ref.at[shard, pl.ds(pl.multiple_of(half * size, size), size), :]
        return view

    rings = [
        Ring(me, c, rows_view(ref, size), ring_s.at[i], ring_r.at[i])
        for i, (ref, size) in enumerate([(wx, 64), (wz, 64), (wo, 512)])
    ]
    ring_x, ring_z, ring_o = rings
    r, q2 = iota((128, 256), 0), iota((128, 256), 1)
    loads[0].wait()
    wx[c] = mm(onehot(q2 == 2 * r), w_in[...]).astype(BF16)
    loads[1].wait()

    e_row = ids[...]
    oh = onehot(iota((8, TOK), 0) == e_row)
    earlier = onehot(iota((TOK, TOK), 0) < iota((TOK, TOK), 1))
    before = mm(oh, earlier)
    p_row = jnp.sum(before * oh.astype(F32), axis=0, keepdims=True).astype(jnp.int32)
    pick_big = onehot(iota((256, TOK), 0) == jnp.where(p_row < 32, e_row * 32 + p_row, -1))
    r128 = iota((128, TOK), 0)
    smallhit = (r128 // 16 == e_row) & (lax.rem(r128, 4) == p_row - 32)
    q128 = lax.rem(r128 // 4, 4)
    smalls = jnp.zeros((128, 512), F32)
    for q in range(4):
        cols = slice(q * 512, q * 512 + 512)
        t = tok[:, cols]
        sbig[:, :, cols] = mm(pick_big, t).astype(BF16).reshape(8, 32, 512)
        smalls = smalls + mm(onehot(smallhit & (q128 == q)), t)
    ssmall[...] = smalls.astype(BF16).reshape(8, 16, 512)

    wz[c] = mm(onehot(q2 == 2 * r + 1), w_in[...]).astype(BF16)
    loads[2].wait()
    loads[3].wait()
    shared = mm(tok[...], w_bc[...]).astype(BF16)
    sb[...] = shared[:, :128]
    sc[...] = shared[:, 128:]
    dt = lax.dot_general(w_dt[...], tok[...], NT, preferred_element_type=F32).astype(BF16)
    extra = jnp.concatenate(
        [dt, damp[...], e_row.astype(BF16), p_row.astype(BF16), jnp.zeros((13, TOK), BF16)], axis=0
    )
    r256, c48 = iota((256, 48), 0), iota((256, 48), 1)
    kind = lax.rem(r256, 16)
    wanted = jnp.where(kind < 2, 2 * (r256 // 16) + kind, jnp.where(kind < 5, 30 + kind, 48))
    saux[...] = mm(onehot(c48 == wanted), extra).astype(BF16).reshape(16, 16, TOK)

    def peer(k):
        return lax.rem(me // 4 + k // 4, 4) * 4 + lax.rem(me + k % 4, 4)

    def to(k):
        return {"device_id": (c, peer(k)), "device_id_type": MESH}

    def slots_to(k):
        g = peer(k)
        return (
            pltpu.make_async_remote_copy(
                sbig.at[g // 2], slots.at[pl.ds(rows_of(me), 32), :],
                ds.at[0, k], dr.at[0, k], **to(k)),
            pltpu.make_async_remote_copy(
                ssmall.at[g // 2], small.at[me], ds.at[1, k], dr.at[1, k], **to(k)),
        )

    def keys_to(k):
        return (
            pltpu.make_async_remote_copy(sb, bb.at[me], ds.at[2, k], dr.at[2, k], **to(k)),
            pltpu.make_async_remote_copy(
                saux.at[peer(k)], aux.at[me], ds.at[3, k], dr.at[3, k], **to(k)),
        )

    def queries_to(k):
        return (pltpu.make_async_remote_copy(sc, bcq.at[me], ds.at[4, k], dr.at[4, k], **to(k)),)

    def start_all(make, some=ORDER):
        for k in some:
            for cp in make(k):
                cp.start()

    def wait_all(make):
        def one(k):
            for cp in make(k):
                cp.wait()
        over(1, N, one)

    pl.semaphore_wait(bar, 2 * (N - 1))
    ring_x.begin()
    start_all(slots_to, ORDER[:4])
    own = [
        pltpu.make_async_copy(sbig.at[me // 2], slots.at[pl.ds(rows_of(me), 32), :], ls.at[1]),
        pltpu.make_async_copy(ssmall.at[me // 2], small.at[me], ls.at[2]),
        pltpu.make_async_copy(sb, bb.at[me], ls.at[3]),
        pltpu.make_async_copy(sc, bcq.at[me], ls.at[4]),
        pltpu.make_async_copy(saux.at[me], aux.at[me], ls.at[5]),
    ]
    for cp in own:
        cp.start()
    over(0, 1, ring_x.step)
    start_all(slots_to, ORDER[4:8])
    over(1, 3, ring_x.step)
    start_all(slots_to, ORDER[8:12])
    over(3, 5, ring_x.step)
    ring_z.begin()
    start_all(slots_to, ORDER[12:])
    over(5, 6, ring_x.step)
    start_all(keys_to, ORDER[:4])
    over(6, 7, ring_x.step)
    start_all(keys_to, ORDER[4:8])
    ring_x.arrive()
    over(0, 1, ring_z.step)
    start_all(keys_to, ORDER[8:12])
    over(1, 2, ring_z.step)
    start_all(keys_to, ORDER[12:])
    for cp in own:
        cp.wait()
    wait_all(slots_to)
    r64, c256 = iota((64, 256), 0), iota((64, 256), 1)
    flat = small[...].reshape(256, 512)
    for q in range(4):
        pickq = onehot(c256 == (r64 // 4) * 16 + q * 4 + lax.rem(r64, 4))
        rows = mm(pickq, flat).astype(BF16)
        slots[256:288, q * 512 : q * 512 + 512] = rows[:32]
        slots[544:576, q * 512 : q * 512 + 512] = rows[32:]

    left288 = left_lanes(288)

    def slab_to(part, k):
        src, dst = (outx, rx) if part == 0 else (outz, rz)
        span = (pl.ds(0, 288), pl.ds(128, 160), pl.ds(0, 128))[part]
        return pltpu.make_async_remote_copy(
            src.at[peer(k), span, :], dst.at[me, span, :], ps_.at[part, k], pr_.at[part, k],
            **to(k))

    def project(half, w, slab, got, between):
        def send(quad):
            for i in range(4):
                k = lax.rem(quad - me // 4 + 4, 4) * 4 + lax.rem(i - lax.rem(me, 4) + 4, 4)

                @pl.when(k != 0)
                def _():
                    slab_to(half, k).start()

        def at(j):
            return lax.rem(2 * j + 1 - j // 2 + me // 4, 4)

        def tile(j):
            quad = at(j)
            cols = pl.ds(pl.multiple_of(quad * 256, 256), 256)
            t2 = mm(slots[...], w[:, :, cols].reshape(WIDTH, 256))
            for i in range(2):
                t = t2[:288, 128 * i : 128 * i + 128]
                b = t2[288:, 128 * i : 128 * i + 128]
                slab[4 * quad + 2 * i] = jnp.where(left288, t, turn(b)).astype(BF16)
                slab[4 * quad + 2 * i + 1] = jnp.where(left288, turn(t), b).astype(BF16)

            @pl.when(j > 0)
            def _():
                send(at(j - 1))

            between(j)

        over(0, 4, tile)
        send(at(3))
        cp = pltpu.make_async_copy(slab.at[me], got.at[me], ls.at[6 + half])
        cp.start()
        return cp

    def ring_between(j):
        @pl.when(lax.rem(j, 2) == 1)
        def _():
            ring_z.step(2 + j // 2)

    own_x = project(0, wx, outx, rx, ring_between)
    start_all(queries_to)
    over(4, 6, ring_z.step)
    own_out.wait()
    ring_o.begin()
    over(6, 7, ring_z.step)
    ring_z.arrive()
    own_z = project(1, wz, outz, rz, lambda j: None)
    for k in ORDER:
        slab_to(2, k).start()
    own_x.wait()
    over(1, N, lambda k: slab_to(0, k).wait())
    wait_all(keys_to)

    left = left_lanes(TOK)
    left1 = left_lanes(1)
    eye = onehot(iota((TOK, TOK), 0) == iota((TOK, TOK), 1))

    def gathered(ref, s8, h):
        o = pl.multiple_of(s8 * 32, 32)
        so = pl.multiple_of(256 + (s8 // 4) * 16, 16)
        parts = []
        for e in range(8):
            parts.append(ref[2 * e + h, pl.ds(o, 32), :])
            parts.append(ref[2 * e + h, pl.ds(so, 16), :])
        return jnp.concatenate(parts, axis=0)

    def back_in_order(ref, s8, p2):
        a0 = mm(p2, gathered(ref, s8, 0))
        a1 = mm(p2, gathered(ref, s8, 1))
        low = jnp.where(left, a0[:TOK], turn(a1[:TOK]))
        high = jnp.where(left, turn(a0[TOK:]), a1[TOK:])
        return low, high

    def places(s):
        cols = lax.dot_general(eye, aux[s], NT, preferred_element_type=F32).astype(jnp.int32)
        e_col, p_col = cols[:, 3:4], cols[:, 4:5]
        target = e_col * 48 + jnp.where(p_col < 32, p_col, p_col + lax.rem(s, 4) * 4)
        return onehot(iota((TOK, 384), 1) == target)

    def unpermute(s8):
        ps[s8, :TOK, :] = places(s8)
        ps[s8, TOK:, :] = places(s8 + 8)
        low, high = back_in_order(rx, s8, ps[s8])
        xs[pl.ds(pl.multiple_of(8 + s8 * TOK, 8), TOK), :] = low
        xs[pl.ds(pl.multiple_of(8 + (s8 + 8) * TOK, 8), TOK), :] = high

    unpermute(7)
    edge_out[...] = xs[3064:3080, :].astype(BF16)
    edge = pltpu.make_async_remote_copy(
        edge_out, edge_in, es.at[0], es.at[1],
        device_id=(lax.rem(c + 1, N), me), device_id_type=MESH)

    def unp(s8, _):
        unpermute(s8)
        return 0

    edge.start()
    lax.fori_loop(0, 7, unp, 0)
    over(0, 1, ring_o.step)
    edge.wait()
    first = jnp.where(c == 0, 0.0, 1.0)
    xs[0:8, :] = edge_in[...].astype(F32)[8:] * first

    state[...] = jnp.zeros((128, 128), F32)
    pre[...] = jnp.zeros((8, 128), F32)
    r2, c2 = iota((384, TOK), 0), iota((384, TOK), 1)
    low_eye = jnp.where(((r2 < TOK) & (c2 <= r2)) | (c2 == r2 - TOK), 1.0, 0.0)
    upper = jnp.where(iota((TOK, TOK), 0) <= iota((TOK, TOK), 1), 1.0, 0.0)

    def states(s, _):
        a = aux[s].astype(F32)
        rows = []
        for h in range(2):
            v = a[h : h + 1] + bias[h]
            rows.append(jnp.maximum(v, 0.0) + jnp.log1p(jnp.exp(-jnp.abs(v))))
        logs = [-(rate[h] * rows[h] + a[2:3]) for h in range(2)]
        rows8 = jnp.concatenate(logs + rows + [jnp.zeros((4, TOK), F32)], axis=0)
        colf = lax.dot_general(low_eye, rows8, NT, precision=HIGHEST, preferred_element_type=F32)
        climb = jnp.dot(rows8, upper, precision=HIGHEST, preferred_element_type=F32)
        clr[s] = climb
        cl = jnp.where(left, colf[:TOK, 0:1], colf[:TOK, 1:2])
        dts = jnp.where(left, colf[TOK:, 2:3], colf[TOK:, 3:4])
        cls[s] = cl
        tot = jnp.where(left1, climb[0:1, TOK - 1 : TOK], climb[1:2, TOK - 1 : TOK])
        full = xs[pl.ds(pl.multiple_of(s * TOK, 8), TOK + 8), :]
        w = conv[3:4, :] * full[8:]
        for k in range(3):
            w = w + conv[k : k + 1, :] * pltpu.roll(full, 3 - k, 0)[8:]
        u = w / (1.0 + jnp.exp(-w))
        us[s] = u
        dtu = dts * u
        dtus[s] = dtu.astype(BF16)
        weighted = (jnp.exp(tot - cl) * dtu).astype(BF16)
        old = state[...]
        ents[s] = old.astype(BF16)
        keys = bb[s]
        state[...] = jnp.exp(tot) * old + lax.dot_general(
            keys, weighted, TN, preferred_element_type=F32
        )
        before = pre[...]
        ys[s] = cl + before[0:1]
        pre[...] = before + tot

        @pl.when(lax.rem(s, 5) == 4)
        def _():
            ring_o.step(1 + s // 5)

        return 0

    lax.fori_loop(0, N, states, 0)
    core = lax.rem(c, 2)
    chip = c // 2
    partner = c + 1 - 2 * core
    near, far = pl.ds(pl.multiple_of(64 * core, 64), 64), pl.ds(pl.multiple_of(64 - 64 * core, 64), 64)

    def in_three(tot):
        t1 = tot.astype(BF16)
        t2 = (tot - t1.astype(F32)).astype(BF16)
        t3 = (tot - t1.astype(F32) - t2.astype(F32)).astype(BF16)
        return jnp.concatenate([t1, t2, t3, jnp.zeros((13, 128), BF16)], axis=0)

    def summed(rows):
        f = rows.astype(F32)
        return f[0:1] + f[1:2] + f[2:3]

    fin_out[0:128, :] = state[...].astype(BF16)
    fin_out[128:144, :] = in_three(pre[0:1])

    def swap(src, dst, sem):
        return pltpu.make_async_remote_copy(
            src, dst, fs.at[sem], fr.at[sem], device_id=(partner, me), device_id_type=MESH)

    swap(fin_out, fin_in, 8).start()

    def chip_to(k):
        return pltpu.make_async_remote_copy(
            chip_out, chips.at[chip], fs.at[k], fr.at[k],
            device_id=(lax.rem(c + 2 * k, N), me), device_id_type=MESH)

    mask = iota((TOK, TOK), 0) >= iota((TOK, TOK), 1)
    over(1, N, lambda k: queries_to(k)[0].wait_recv())

    def inside(s, _):
        queries = bcq[s]
        gram = lax.dot_general(queries, bb[s], NT, preferred_element_type=F32)
        cl = cls[s]
        cr = clr[s]
        dtu = dtus[s]
        halves = []
        for h in range(2):
            d = cl[:, 64 * h : 64 * h + 1] - cr[h : h + 1]
            m = jnp.exp(jnp.where(mask, d, -1e30)) * gram
            halves.append(mm(m.astype(BF16), dtu))
        inter = mm(queries, ents[s]) * jnp.exp(cl)
        skip = jnp.where(left1, dskip[0], dskip[1])
        us[s] = jnp.where(left, halves[0], halves[1]) + inter + skip * us[s]

        @pl.when(lax.rem(s, 5) == 4)
        def _():
            ring_o.step(4 + s // 5)

        return 0

    lax.fori_loop(0, 4, inside, 0)
    swap(fin_out, fin_in, 8).wait()
    mine_t, other_t = pre[0:1], summed(fin_in[128:144, :])
    mine_s, other_s = state[near, :], fin_in[near, :].astype(F32)
    even = core == 0
    chip_out[0:64, :] = (
        jnp.exp(jnp.where(even, other_t, mine_t)) * jnp.where(even, mine_s, other_s)
        + jnp.where(even, other_s, mine_s)
    ).astype(BF16)
    chip_out[64:80, :] = in_three(mine_t + other_t)
    over(1, 8 - chip, lambda k: chip_to(k).start())
    lax.fori_loop(4, N, inside, 0)
    over(1, 8 - chip, lambda k: chip_to(k).wait_send())
    over(1, chip + 1, lambda k: chip_to(k).wait_recv())
    half_out[...] = jnp.zeros((64, 128), F32)

    def lap(i):
        half_out[...] = (
            jnp.exp(summed(chips[i, 64:80, :])) * half_out[...] + chips[i, 0:64, :].astype(F32)
        )

    over(0, chip, lap)
    swap(half_out, half_in, 9).start()
    state[near, :] = half_out[...]
    swap(half_out, half_in, 9).wait()
    state[far, :] = half_in[...]
    state[...] = jnp.where(
        even, state[...], jnp.exp(other_t) * state[...] + fin_in[0:128, :].astype(F32)
    )
    incoming = state[...].astype(BF16)
    rb, cb = iota((128, 128), 0), iota((128, 128), 1)
    means = jnp.where(rb // 64 == cb // 64, 1.0 / 64, 0.0)

    def stage(j, k):
        span = pl.ds(256, 32) if j == 4 else pl.ds(64 * j, 64)
        return pltpu.make_async_remote_copy(
            out.at[peer(k), span, :], back.at[me, span, :], ks.at[j, k], kr.at[j, k], **to(k))

    def launch(j):
        for k in ORDER:
            stage(j, k).start()

    def finish(s, z):
        y = us[s] + jnp.exp(ys[s]) * mm(bcq[s], incoming)
        v = y * (z / (1.0 + jnp.exp(-z)))
        ms = jnp.dot(v * v, means, precision=HIGHEST, preferred_element_type=F32)
        normed = (v * lax.rsqrt(ms + 1e-5) * gain[...]).astype(BF16)
        a = aux[s].astype(F32).astype(jnp.int32)
        e_row, p_row = a[3:4], a[4:5]
        target = e_row * 48 + jnp.where(p_row < 32, p_row, p_row + lax.rem(s, 4) * 4)
        return mm(onehot(iota((384, TOK), 0) == target), normed)

    left384 = left_lanes(384)

    def closing(s8, _):
        zl, zh = back_in_order(rz, s8, ps[s8])
        tl = finish(s8, zl)
        th = finish(s8 + 8, zh)
        for h in range(2):
            v = jnp.where(left384, tl, turn(th)) if h == 0 else jnp.where(left384, turn(tl), th)
            fresh = lax.rem(s8, 4) == 0
            total = jnp.where(fresh, 0.0, acc[h]) + v
            acc[h] = total
            for e in range(8):
                out[2 * e + h, pl.ds(pl.multiple_of(s8 * 32, 32), 32), :] = v[
                    e * 48 : e * 48 + 32
                ].astype(BF16)
                out[2 * e + h, pl.ds(pl.multiple_of(256 + (s8 // 4) * 16, 16), 16), :] = total[
                    e * 48 + 32 : e * 48 + 48
                ].astype(BF16)
        return 0

    acc[...] = jnp.zeros((2, 384, 128), F32)
    own_z.wait()
    over(1, N, lambda k: slab_to(1, k).wait_recv())
    lax.fori_loop(4, 6, closing, 0)
    launch(2)
    lax.fori_loop(6, 8, closing, 0)
    launch(3)
    over(1, N, lambda k: slab_to(2, k).wait_recv())
    lax.fori_loop(0, 2, closing, 0)
    launch(0)
    lax.fori_loop(2, 4, closing, 0)
    launch(1)
    launch(4)
    own_back = pltpu.make_async_copy(out.at[me], back.at[me], ls.at[8])
    own_back.start()


    def big_to(part, q, k):
        cols = pl.ds(pl.multiple_of(q * 512, 512), 512)
        return pltpu.make_async_remote_copy(
            o.at[pl.ds(rows_of(peer(k)), 32), cols], big.at[me, :, cols],
            qs.at[q, k], qr.at[q, k], **to(k))

    def small_to(k):
        return pltpu.make_async_remote_copy(
            osm.at[peer(k)], rsmall.at[me], qs.at[4, k], qr.at[4, k], **to(k))

    ring_o.arrive()
    own_back.wait()
    for j in (2, 3, 0, 1, 4):
        over(1, N, lambda k: stage(j, k).wait())
    for j in range(8):
        even = back[2 * j].astype(F32)
        odd = back[2 * j + 1].astype(F32)
        a[:288, 128 * j : 128 * j + 128] = jnp.where(left288, even, turn(odd)).astype(BF16)
        a[288:, 128 * j : 128 * j + 128] = jnp.where(left288, turn(even), odd).astype(BF16)
    r256b, c64 = iota((256, 64), 0), iota((256, 64), 1)

    def quarter(q, total):
        for i in range(2):
            t = mm(a[...], jnp.concatenate([wo[4 * q + 2 * i], wo[4 * q + 2 * i + 1]], axis=1))
            o[:, pl.ds(pl.multiple_of(q * 512 + i * 256, 256), 256)] = t.astype(BF16)
        for k in ORDER:
            big_to(0, q, k).start()
        cols = pl.ds(pl.multiple_of(q * 512, 512), 512)
        rows = jnp.concatenate([o[256:288, cols], o[544:576, cols]], axis=0)
        place = onehot(
            (lax.rem(r256b // 4, 4) == q) & (c64 == (r256b // 16) * 4 + lax.rem(r256b, 4))
        )
        return total + mm(place, rows)

    total = lax.fori_loop(0, 4, quarter, jnp.zeros((256, 512), F32))
    osm[...] = total.astype(BF16).reshape(16, 16, 512)
    for k in ORDER:
        small_to(k).start()
    own = [
        pltpu.make_async_copy(o.at[pl.ds(rows_of(me), 32), :], big.at[me], ls.at[9]),
        pltpu.make_async_copy(osm.at[me], rsmall.at[me], ls.at[10]),
    ]
    for cp in own:
        cp.start()
    mine = lax.dot_general(
        eye, jnp.concatenate([e_row, p_row] + [jnp.zeros_like(e_row)] * 6, axis=0).astype(BF16),
        NT, preferred_element_type=F32,
    ).astype(jnp.int32)
    e_col, p_col = mine[:, 0:1], mine[:, 1:2]
    c512 = iota((TOK, 512), 1)
    pick = onehot((c512 // 64 == e_col) & (lax.rem(c512, 32) == p_col))
    c256b = iota((TOK, 256), 1)
    for ring in rings:
        ring.sent()
    over(1, N, lambda k: queries_to(k)[0].wait_send())
    for part in (1, 2):
        over(1, N, lambda k: slab_to(part, k).wait_send())
    for cp in own:
        cp.wait()
    for q in range(4):
        over(1, N, lambda k: big_to(0, q, k).wait())
        cols = slice(q * 512, q * 512 + 512)
        res[:, cols] = mm(pick, big[:, :, cols].reshape(512, 512)).astype(BF16)
    over(1, N, lambda k: small_to(k).wait())
    late = rsmall[...].reshape(256, 512)
    for q in range(4):
        pickq = onehot(
            (c256b // 32 == e_col) & (lax.rem(c256b, 16) == q * 4 + p_col - 32) & (p_col >= 32)
        )
        cols = slice(q * 512, q * 512 + 512)
        res[:, cols] = (res[:, cols].astype(F32) + mm(pickq, late)).astype(BF16)


VM = pl.BlockSpec(memory_space=pltpu.VMEM)
SM = pl.BlockSpec(memory_space=pltpu.SMEM)
DMA = pltpu.SemaphoreType.DMA
ANY = pl.BlockSpec(memory_space=pl.ANY)


def on_device(
    tokens, expert_ids, damping, in_weight, out_weight, w_bc, w_dt, rate, dt_bias, d_skip,
    gain, conv_weight,
):
    def v(*dims, dtype=BF16):
        return pltpu.VMEM(dims, dtype)

    return pl.pallas_call(
        layer_kernel,
        name="layer",
        out_shape=jax.ShapeDtypeStruct((TOK, WIDTH), BF16),
        in_specs=[ANY, VM, VM] + [ANY] * 4 + [SM] * 3 + [VM] * 2,
        out_specs=VM,
        scratch_shapes=[
            v(N, 128, 1024), v(N, 128, 1024), v(N, 1024, 128), v(576, WIDTH),
            v(8, 32, WIDTH), v(8, 16, 512), v(TOK, 128), v(TOK, 128), v(N, 16, TOK),
            v(N, 16, 512), v(N, TOK, 128), v(N, TOK, 128), v(N, 16, TOK),
            v(N, 288, 128), v(N, 288, 128), v(N, 288, 128), v(N, 288, 128),
            v(3080, 128, dtype=F32), v(8, 384, 384), v(N, TOK, 128, dtype=F32), v(N, TOK, 128),
            v(N, TOK, 128, dtype=F32), v(N, 8, TOK, dtype=F32), v(N, 128, 128),
            v(N, TOK, 128, dtype=F32), v(8, 128, dtype=F32), v(128, 128, dtype=F32),
            v(16, 128), v(16, 128), v(144, 128), v(144, 128), v(80, 128), v(8, 80, 128),
            v(64, 128, dtype=F32), v(64, 128, dtype=F32), v(2, 384, 128, dtype=F32),
            v(N, 288, 128), v(N, 288, 128), v(576, 1024), v(576, WIDTH), v(N, 16, 512),
            v(N, 32, WIDTH), v(N, 16, 512),
            v(TOK, WIDTH), v(256, 1024), v(WIDTH, 256), v(32, WIDTH),
            DMA((3, 32)), DMA((3, 32)), DMA((5, N)), DMA((5, N)), DMA((3, N)), DMA((3, N)),
            DMA((2,)), DMA((N,)), DMA((N,)), DMA((5, N)), DMA((5, N)),
            DMA((5, N)), DMA((5, N)), DMA((15,)),
        ],
        compiler_params=pltpu.CompilerParams(
            collective_id=0, has_side_effects=True, vmem_limit_bytes=VLIM
        ),
    )(
        tokens, expert_ids.reshape(1, TOK), damping.reshape(1, TOK),
        in_weight.reshape(256, 1024), out_weight[0], w_bc, w_dt, rate, dt_bias, d_skip,
        gain.reshape(1, 128), conv_weight,
    )


def solution(mesh):
    placed = (
        P(("ctx", "exp"), None), P(("ctx", "exp"), None), P(("ctx", "exp")),
        P("exp", "ctx", None, None), P("exp", None, "ctx"), P(), P(),
        P("exp"), P("exp"), P("exp"), P("exp"), P(None, "exp"),
    )
    return jax.shard_map(
        on_device, mesh=mesh, in_specs=placed, out_specs=P(("ctx", "exp"), None), check_vma=False
    )
```
